1024 devices in a mesh: dp: 2 (over core), ctx: 128 (over z, x), tp: 4 (over y).
Axes of the slice: x: 4, y: 4, z: 32, core: 2. Of those that a mesh axis runs over, the one named last changes fastest.
Arguments:
- queries: bfloat16 [2, 16384, 2048], P('dp', 'ctx', 'tp'), may hold values from -48 to 48
- key_rows: bfloat16 [2, 16384, 1024], P('dp', 'ctx', 'tp'), may hold values from -6 to 6
- values: bfloat16 [2, 16384, 1024], P('dp', 'ctx', 'tp'), may hold values from -6 to 6
- grad_out: bfloat16 [2, 16384, 2048], P('dp', 'ctx', 'tp'), may hold values from -6 to 6
- lengths: int32 [2, 8], replicated, may hold values from 1 to 8192, 16384 in all within a row
- pair_swap: int32 [128], P('ctx'), may hold values from 0 to 1
Outputs:
- attn_out: bfloat16 [2, 16384, 2048], P('dp', ('ctx', 'tp'))
- grad_query: bfloat16 [2, 16384, 2048], P('dp', 'ctx', 'tp')
- grad_keys: bfloat16 [2, 16384, 1024], P('dp', 'ctx', 'tp')
- grad_values: bfloat16 [2, 16384, 1024], P('dp', 'ctx', 'tp')
The draws below stay inside these ranges and needn't reach their ends.
All inputs are finite; a program needn't handle non-finite values.
Results may differ from the reference program's by a relative error of at most 0.012.
Values may be sent and summed in bfloat16 or wider, within the bound.
A program may use at most 32 MiB of HBM per device.

```python
import math
import jax
import jax.numpy as jnp
import numpy as np
from jax import lax

HD = 128
REP = 2
W = 512
TOK_DEV = 128
ROLLS = 8
KV_HEADS = 8
Q_HEADS = 16
PACK_LEN = 16384
PACKS = 2
MOST_LEN = 8192
N_CTX = 128


def draw_key_rows(key, part):
    full_shape = (PACKS, PACK_LEN, KV_HEADS * HD)
    return jnp.clip(jax.random.normal(jax.random.fold_in(key, 41), full_shape, jnp.float32), -6.0, 6.0).astype(jnp.bfloat16)


def draw_queries(key, part):
    full_shape = (PACKS, PACK_LEN, Q_HEADS * HD)
    return jnp.clip(2.0 * jax.random.normal(jax.random.fold_in(key, 67), full_shape, jnp.float32), -12.0, 12.0).astype(jnp.bfloat16)


def set_ends(drawn, own_key, least, high):
    longest = drawn.shape.index(max(drawn.shape))
    spots = []
    for shift in (0, 1):
        where = [jax.random.randint(jax.random.fold_in(own_key, axis), (), 0, length) for axis, length in enumerate(drawn.shape)]
        where[longest] = (where[longest] + shift) % drawn.shape[longest]
        spots.append(tuple(where))
    return drawn.at[spots[0]].set(least).at[spots[1]].set(high)


def block_levels(key, dims, cuts, smallest, largest):
    level, own = 1.0, jax.random.fold_in(key, 6)
    for dim, parts in cuts:
        draws = jnp.exp(jax.random.uniform(jax.random.fold_in(own, dim), (parts,), jnp.float32, smallest / len(cuts), largest / len(cuts)))
        level = level * jnp.repeat(draws, dims[dim] // parts).reshape([-1 if axis == dim else 1 for axis in range(len(dims))])
    return level


def length_profile(number_of, total, bound, skew):
    weights = [(1 << 20) // math.isqrt(standing ** skew) + 1 for standing in range(2, number_of + 1)]
    rest, holding = total - bound - (number_of - 1), [1] * (number_of - 1)
    while rest > 0:
        free = [i for i in range(number_of - 1) if holding[i] < bound]
        pool, budget = sum([weights[i] for i in free]), rest
        for i in free:
            addition = min(bound - holding[i], max(1, budget * weights[i] // pool), rest)
            holding[i] = holding[i] + addition
            rest = rest - addition
    return np.array([bound] + holding)


def uneven_parts(stream_key, amount, total, bound, lean):
    if amount == 2:
        one = jax.random.randint(stream_key, (), max(1, total - bound), min(bound, total - 1) + 1)
        return jnp.stack([one, total - one])
    sizes = jnp.asarray(length_profile(amount, total, bound, lean), jnp.int32)
    pairs = (amount - 1) // 2
    donor, taker = sizes[1:1 + 2 * pairs:2], sizes[2:2 + 2 * pairs:2]
    slack = jnp.minimum(donor - 1, bound - taker)
    shifted = jax.random.randint(jax.random.fold_in(stream_key, 1), (pairs,), 0, 1 << 20) % (slack + 1)
    sizes = sizes.at[1:1 + 2 * pairs:2].set(donor - shifted).at[2:2 + 2 * pairs:2].set(taker + shifted)
    return sizes[jax.random.permutation(jax.random.fold_in(stream_key, 2), amount)]


def normal_values(own_key, dims, scale, most, cuts=(), kind=jnp.bfloat16):
    values = scale * jax.random.normal(own_key, dims, jnp.float32)
    if cuts:
        values = values * block_levels(own_key, dims, cuts, -0.22, 0.18)
    return jnp.clip(values, -most, most).astype(kind)


def setup_inputs(seed: int = 0) -> dict:
    key_list = jax.random.split(jax.random.key(seed), 7)
    return {
        "queries": draw_queries(jax.random.fold_in(key_list[6], 71), 0),
        "key_rows": draw_key_rows(jax.random.fold_in(key_list[6], 71), 0),
        "values": normal_values(key_list[2], (PACKS, PACK_LEN, KV_HEADS * HD), 1.0, 6.0, ((0, 2), (1, 128), (2, 4))),
        "grad_out": normal_values(key_list[3], (PACKS, PACK_LEN, Q_HEADS * HD), 1.0, 6.0, ((0, 2), (1, 128), (2, 4))),
        "lengths": jax.vmap(lambda own: uneven_parts(own, ROLLS, PACK_LEN, MOST_LEN, 2))(jax.random.split(key_list[4], PACKS)).reshape((PACKS, ROLLS)).astype(jnp.int32),
        "pair_swap": set_ends(jax.random.randint(key_list[5], (N_CTX,), 0, 2), jax.random.fold_in(key_list[5], 1), 0, 1).astype(jnp.int32),
    }


SCALE = 168.0 ** -0.5
NEGATIVE = -1.0e30


def window_mask(start_pos, row_count, key_count, run_ends):
    q_pos = start_pos + jnp.arange(row_count, dtype=jnp.int32)
    k_pos = start_pos - (key_count - row_count) + jnp.arange(key_count, dtype=jnp.int32)
    q_seg = jnp.sum((q_pos[:, None] >= run_ends[None, :]).astype(jnp.int32), axis=1)
    k_seg = jnp.sum((k_pos[:, None] >= run_ends[None, :]).astype(jnp.int32), axis=1)
    spacing = q_pos[:, None] - k_pos[None, :]
    return (spacing >= 0) & (spacing < W) & (k_pos[None, :] >= 0) & (q_seg[:, None] == k_seg[None, :])


def group_core(q_part, k_part, v_part, g_part, allowed, repeat):
    row_count = q_part.shape[0]
    width = k_part.shape[1]
    q_heads = q_part.reshape(row_count, repeat, width).astype(jnp.float32)
    g_heads = g_part.reshape(row_count, repeat, width).astype(jnp.float32)
    k_full = k_part.astype(jnp.float32)
    v_full = v_part.astype(jnp.float32)
    scores = jnp.einsum("qrd,kd->rqk", q_heads, k_full) * SCALE
    scores = jnp.where(allowed[None], scores, NEGATIVE)
    row_peak = jnp.max(scores, axis=2, keepdims=True)
    weights = jnp.exp(scores - row_peak)
    probs = weights / jnp.sum(weights, axis=2, keepdims=True)
    probs_low = probs.astype(jnp.bfloat16)
    probs_wide = probs_low.astype(jnp.float32)
    attended = jnp.einsum("rqk,kd->qrd", probs_wide, v_full).astype(jnp.bfloat16).reshape(row_count, repeat * width)
    dprob = jnp.einsum("qrd,kd->rqk", g_heads, v_full)
    delta = jnp.sum(probs * dprob, axis=2, keepdims=True)
    dscore = (probs * (dprob - delta)).astype(jnp.bfloat16).astype(jnp.float32)
    grad_q = (jnp.einsum("rqk,kd->qrd", dscore, k_full) * SCALE).astype(jnp.bfloat16).reshape(row_count, repeat * width)
    grad_k = jnp.einsum("rqk,qrd->kd", dscore, q_heads) * SCALE
    grad_v = jnp.einsum("rqk,qrd->kd", probs_wide, g_heads)
    return attended, grad_q, grad_k, grad_v


def attend_groups(q_part, k_part, v_part, g_part, allowed):
    group_count = k_part.shape[1] // HD
    pieces = []
    for group_idx in range(group_count):
        q_cols = slice(group_idx * REP * HD, (group_idx + 1) * REP * HD)
        k_cols = slice(group_idx * HD, (group_idx + 1) * HD)
        pieces.append(group_core(q_part[:, q_cols], k_part[:, k_cols], v_part[:, k_cols], g_part[:, q_cols], allowed, REP))
    return tuple(jnp.concatenate([piece[member] for piece in pieces], axis=1) for member in range(4))


def reorder(stored, pair_swap):
    blocks = stored.reshape((PACKS, N_CTX, TOK_DEV, stored.shape[-1]))
    flags = (pair_swap == 1).reshape((1, N_CTX, 1, 1))
    return jnp.where(flags, blocks[::-1], blocks).reshape(stored.shape)


def pack_attention(q_pack, k_pack, v_pack, g_pack, lengths_row):
    run_ends = jnp.cumsum(lengths_row)
    kv_cols = k_pack.shape[1]
    padding = jnp.zeros((W, kv_cols), k_pack.dtype)
    k_padded = jnp.concatenate([padding, k_pack], axis=0)
    v_padded = jnp.concatenate([padding, v_pack], axis=0)

    def block_step(carried, block_idx):
        acc_k, acc_v = carried
        start_pos = (block_idx * TOK_DEV).astype(jnp.int32)
        q_block = lax.dynamic_slice_in_dim(q_pack, start_pos, TOK_DEV, 0)
        g_block = lax.dynamic_slice_in_dim(g_pack, start_pos, TOK_DEV, 0)
        k_block = lax.dynamic_slice_in_dim(k_padded, start_pos, TOK_DEV + W, 0)
        v_block = lax.dynamic_slice_in_dim(v_padded, start_pos, TOK_DEV + W, 0)
        allowed = window_mask(start_pos, TOK_DEV, TOK_DEV + W, run_ends)
        attended, grad_q, grad_k, grad_v = attend_groups(q_block, k_block, v_block, g_block, allowed)
        acc_k = lax.dynamic_update_slice_in_dim(acc_k, lax.dynamic_slice_in_dim(acc_k, start_pos, TOK_DEV + W, 0) + grad_k, start_pos, 0)
        acc_v = lax.dynamic_update_slice_in_dim(acc_v, lax.dynamic_slice_in_dim(acc_v, start_pos, TOK_DEV + W, 0) + grad_v, start_pos, 0)
        return (acc_k, acc_v), (attended, grad_q)

    zeros_acc = jnp.zeros((W + PACK_LEN, kv_cols), jnp.float32)
    block_ids = jnp.arange(PACK_LEN // TOK_DEV, dtype=jnp.int32)
    (acc_k, acc_v), (attended, grad_q) = lax.scan(block_step, (zeros_acc, zeros_acc), block_ids)
    return (attended.reshape(PACK_LEN, -1), grad_q.reshape(PACK_LEN, -1),
            acc_k[W:].astype(jnp.bfloat16), acc_v[W:].astype(jnp.bfloat16))


def reference(queries, key_rows, values, grad_out, lengths, pair_swap):
    pack_q = reorder(queries, pair_swap)
    pack_k = reorder(key_rows, pair_swap)
    pack_v = reorder(values, pair_swap)
    pack_g = reorder(grad_out, pair_swap)
    results = [pack_attention(pack_q[pack_idx], pack_k[pack_idx], pack_v[pack_idx], pack_g[pack_idx], lengths[pack_idx]) for pack_idx in range(PACKS)]
    attn_out = jnp.stack([item[0] for item in results])
    grad_query = jnp.stack([item[1] for item in results])
    grad_keys = jnp.stack([item[2] for item in results])
    grad_values = jnp.stack([item[3] for item in results])
    return (attn_out, grad_query, grad_keys, grad_values)
```

```python
import functools

import jax
import jax.numpy as jnp
from jax import lax
from jax.experimental import pallas as pl
from jax.experimental.pallas import tpu as pltpu
from jax.sharding import PartitionSpec as P

HD = 128
REP = 2
W = 512
BLK = 128
REACH = W // BLK
NX = 4
QW = REP * HD
QL = REP * BLK

SCALE = 168.0 ** (-0.5)
NEGATIVE = -1e30
MESH = pl.DeviceIdType.MESH
NT = (((1,), (1,)), ((), ()))
TN = (((0,), (0,)), ((), ()))
NN = (((1,), (0,)), ((), ()))


def mm(a, b, dims):
    return lax.dot_general(a, b, dims, preferred_element_type=jnp.float32)


def kernel(
    n_ctx, n_tp,
    q_ref, k_ref, v_ref, g_ref, len_ref, swap_ref,
    ao_ref, gq_ref, gk_ref, gv_ref,
    kb0, kb1, kb2, kb3, kb4, vb0, vb1, vb2, vb3, vb4, qb, gb, flags,
    ks, vs, qs, gs, sc, dp, pb, dsb,
    ob, dqb, part, own, mate, near, far, hub, relay,
    loc_sem, send_sem, rk_sem, rv_sem, rq_sem, rf_sem, out_sem, pd_sem, hub_sem,
):
    kb = (kb0, kb1, kb2, kb3, kb4)
    vb = (vb0, vb1, vb2, vb3, vb4)
    p = lax.axis_index("dp")
    c = lax.axis_index("ctx")
    y = lax.axis_index("tp")
    other = 1 - p
    x = lax.rem(c, NX)
    ahead = lax.rem(c + NX, n_ctx)
    behind = lax.rem(c + n_ctx - NX, n_ctx)

    barrier = pltpu.get_barrier_semaphore()
    partners = [(other, c, y)]
    for d in range(1, NX):
        for j in range(2):
            partners.append((j, c - x + lax.rem(x + d, NX), y))
    for j in range(2):
        partners.append((j, ahead, y))
        partners.append((j, behind, y))
    for d in range(1, n_tp):
        for j in range(2):
            partners.append((j, c, lax.rem(y + d, n_tp)))
    for dev in partners:
        pl.semaphore_signal(barrier, inc=1, device_id=dev, device_id_type=MESH)
    pl.semaphore_wait(barrier, len(partners))

    count = [0]
    waits = []

    def remote(src, dst, recv, dev, cond=None):
        sem = send_sem.at[count[0]]
        count[0] += 1
        cp = pltpu.make_async_remote_copy(
            src_ref=src, dst_ref=dst, send_sem=sem, recv_sem=recv,
            device_id=dev, device_id_type=MESH,
        )
        if cond is None:
            cp.start()
        else:
            @pl.when(cond)
            def _():
                cp.start()
        waits.append((cp, cond))
        return cp

    def arrived(ref, sem):
        pltpu.make_async_copy(ref, ref, sem).wait()

    def cols(ref, j, width):
        return ref.at[0, :, pl.ds(pl.multiple_of(j * width, width), width)]

    mine = (other, c, y)
    remote(cols(k_ref, other, HD), kb0.at[p], rk_sem.at[0], mine)
    remote(cols(q_ref, other, QW), qb.at[p], rq_sem.at[0], mine)
    for j in range(2):
        remote(cols(k_ref, j, HD), kb4.at[p], rk_sem.at[4], (j, ahead, y))
    remote(cols(v_ref, other, HD), vb0.at[p], rv_sem.at[0], mine)
    remote(cols(g_ref, other, QW), gb.at[p], rq_sem.at[1], mine)
    for j in range(2):
        remote(cols(v_ref, j, HD), vb4.at[p], rv_sem.at[4], (j, ahead, y))
    local = [
        pltpu.make_async_copy(cols(k_ref, p, HD), kb0.at[p], loc_sem.at[0]),
        pltpu.make_async_copy(cols(q_ref, p, QW), qb.at[p], loc_sem.at[1]),
        pltpu.make_async_copy(cols(v_ref, p, HD), vb0.at[p], loc_sem.at[2]),
        pltpu.make_async_copy(cols(g_ref, p, QW), gb.at[p], loc_sem.at[3]),
        pltpu.make_async_copy(swap_ref, flags.at[0], loc_sem.at[4]),
    ]
    for cp in local:
        cp.start()
    remote(swap_ref, flags.at[4], rf_sem.at[4], (p, ahead, y))
    for d in range(1, NX):
        remote(swap_ref, flags.at[d], rf_sem.at[d], (p, lax.rem(c + d, n_ctx), y), x + d < NX)
    for src, dst, sem in ((k_ref, kb, rk_sem), (v_ref, vb, rv_sem)):
        for d in (1, 3, 2):
            ok = x + d < NX
            for j in range(2):
                remote(cols(src, j, HD), dst[d].at[p], sem.at[d], (j, lax.rem(c + d, n_ctx), y), ok)

    lane = lax.broadcasted_iota(jnp.int32, (1, BLK), 1)
    pos = c * BLK + lane
    lows = []
    for pi in range(2):
        low = jnp.maximum(pos - (W - 1), 0)
        end = jnp.int32(0)
        for r in range(len_ref.shape[1]):
            end = end + len_ref[pi, r]
            low = jnp.maximum(low, jnp.where(pos >= end, end, 0))
        lows.append(jnp.concatenate([low] * REP, axis=1) - c * BLK)
    lane2 = jnp.concatenate([lane] * REP, axis=1)
    row_id = lax.broadcasted_iota(jnp.int32, (BLK, QL), 0)

    def pick(ref, swapped, pi):
        a, b = ref[pi], ref[1 - pi]
        return jnp.where(swapped, b, a)

    def take(d):
        swapped = flags[d, 0] == 1
        for pi in range(2):
            key = pick(kb[d], swapped, pi)
            ks[pi, d] = key
            s = mm(key, qs[pi], NT) * SCALE
            ok = row_id - d * BLK >= lows[pi]
            if d == 0:
                ok = ok & (row_id <= lane2)
            sc[pi, d] = jnp.where(ok, s, NEGATIVE)

    def take_v(d):
        swapped = flags[d, 0] == 1
        for pi in range(2):
            val = pick(vb[d], swapped, pi)
            vs[pi, d] = val
            dp[pi, d] = mm(val, gs[pi], NT)

    for cp in local:
        cp.wait()
    swapped = flags[0, 0] == 1
    arrived(qb.at[other], rq_sem.at[0])
    for pi in range(2):
        t = pick(qb, swapped, pi)
        for r in range(REP):
            qs[pi, r * BLK:(r + 1) * BLK] = t[:, r * HD:(r + 1) * HD]
    arrived(kb0.at[other], rk_sem.at[0])
    take(0)
    arrived(gb.at[other], rq_sem.at[1])
    for pi in range(2):
        t = pick(gb, swapped, pi)
        for r in range(REP):
            gs[pi, r * BLK:(r + 1) * BLK] = t[:, r * HD:(r + 1) * HD]
    arrived(vb0.at[other], rv_sem.at[0])
    take_v(0)

    for buf, dst, sem in ((kb, kb, rk_sem), (vb, vb, rv_sem)):
        arrived(buf[4], sem.at[4])
        for e in (1, 3, 2):
            ok = x >= e
            remote(buf[4], dst[4 - e], sem.at[4 - e], (p, lax.rem(c + n_ctx - e, n_ctx), y), ok)
    arrived(flags.at[4], rf_sem.at[4])
    for e in range(1, NX):
        remote(flags.at[4], flags.at[4 - e], rf_sem.at[4 - e], (p, lax.rem(c + n_ctx - e, n_ctx), y), x >= e)
    take(4)
    take_v(4)
    for d in (1, 2, 3):
        arrived(flags.at[d], rf_sem.at[d])
        arrived(kb[d], rk_sem.at[d])
        take(d)
    for d in (1, 2, 3):
        arrived(vb[d], rv_sem.at[d])
        take_v(d)

    for pi in range(2):
        top = jnp.max(sc[pi, 0], axis=0, keepdims=True)
        for d in range(1, REACH + 1):
            top = jnp.maximum(top, jnp.max(sc[pi, d], axis=0, keepdims=True))
        total = jnp.zeros((1, QL), jnp.float32)
        for d in range(REACH + 1):
            e = jnp.exp(sc[pi, d] - top)
            sc[pi, d] = e
            total = total + jnp.sum(e, axis=0, keepdims=True)
        inv = 1.0 / total
        delta = jnp.zeros((1, QL), jnp.float32)
        for d in range(REACH + 1):
            pr = sc[pi, d] * inv
            sc[pi, d] = pr
            pb[pi, d] = pr.astype(jnp.bfloat16)
            delta = delta + jnp.sum(pr * dp[pi, d], axis=0, keepdims=True)
        for d in range(REACH + 1):
            dsb[pi, d] = (sc[pi, d] * (dp[pi, d] - delta)).astype(jnp.bfloat16)

    def partial(d, dst):
        for pi in range(2):
            dk = mm(dsb[pi, d], qs[pi], NN) * SCALE
            dv = mm(pb[pi, d], gs[pi], NN)
            dst(pi, dk, dv)

    for d in (3, 2, 1):
        def put(pi, dk, dv, d=d):
            part[d, pi, 0] = dk.astype(jnp.bfloat16)
            part[d, pi, 1] = dv.astype(jnp.bfloat16)
        partial(d, put)
        dev = lax.rem(c + n_ctx - d, n_ctx)
        for pi in range(2):
            remote(part.at[d, pi], near.at[d - 1, p], pd_sem.at[d], (pi, dev, y), x >= d)
        remote(part.at[d], relay.at[NX - d - 1], hub_sem.at[NX - d], (p, c + NX - d, y), x < d)

    def put4(pi, dk, dv):
        hub[pi, 0] = dk
        hub[pi, 1] = dv
    partial(4, put4)

    def put0(pi, dk, dv):
        own[pi, 0] = dk
        own[pi, 1] = dv
    partial(0, put0)
    remote(own.at[other], mate, pd_sem.at[0], mine)

    for pi in range(2):
        o = mm(pb[pi].reshape(-1, QL), vs[pi].reshape(-1, HD), TN).astype(jnp.bfloat16)
        for r in range(REP):
            ob[pi, :, r * HD:(r + 1) * HD] = o[r * BLK:(r + 1) * BLK]
    share = BLK // n_tp
    width = REP * HD
    at = pl.ds(pl.multiple_of((y * 2 + p) * width, width), width)
    for dt in range(n_tp):
        t = lax.rem(y + dt, n_tp)
        rows = pl.ds(pl.multiple_of(t * share, share), share)
        for dj in range(2):
            pi = p if dj == 0 else other
            if dt == 0 and dj == 0:
                keep = pltpu.make_async_copy(ob.at[pi, rows], ao_ref.at[0, :, at], loc_sem.at[5])
                keep.start()
            else:
                remote(ob.at[pi, rows], ao_ref.at[0, :, at], out_sem.at[0], (pi, c, t))
    for pi in range(2):
        o = (mm(dsb[pi].reshape(-1, QL), ks[pi].reshape(-1, HD), TN) * SCALE).astype(jnp.bfloat16)
        for r in range(REP):
            dqb[pi, :, r * HD:(r + 1) * HD] = o[r * BLK:(r + 1) * BLK]
    keep_q = pltpu.make_async_copy(dqb.at[p], cols(gq_ref, p, QW), loc_sem.at[6])
    keep_q.start()
    remote(dqb.at[other], cols(gq_ref, p, QW), out_sem.at[1], mine)

    for e in range(1, NX):
        @pl.when(x >= e)
        def _():
            arrived(relay.at[e - 1], hub_sem.at[e])
            for pi in range(2):
                for s in range(2):
                    hub[pi, s] = hub[pi, s] + relay[e - 1, pi, s].astype(jnp.float32)
    for pi in range(2):
        for s in range(2):
            part[4, pi, s] = hub[pi, s].astype(jnp.bfloat16)
    for pi in range(2):
        remote(part.at[4, pi], far.at[p], pd_sem.at[4], (pi, behind, y))

    arrived(mate, pd_sem.at[0])
    for d in range(1, NX):
        @pl.when(x + d < NX)
        def _():
            arrived(near.at[d - 1], pd_sem.at[d])
            for s in range(2):
                own[p, s] = own[p, s] + near[d - 1, p, s].astype(jnp.float32)
                mate[s] = mate[s] + near[d - 1, other, s].astype(jnp.float32)
    arrived(far, pd_sem.at[4])
    for s, out in ((0, gk_ref), (1, gv_ref)):
        for j, src in ((p, own[p, s]), (other, mate[s])):
            out[0, :, pl.ds(pl.multiple_of(j * HD, HD), HD)] = (
                src + far[j, s].astype(jnp.float32)
            ).astype(jnp.bfloat16)

    keep.wait()
    keep_q.wait()
    arrived(ao_ref.at[0, :, pl.ds(0, (2 * n_tp - 1) * width)], out_sem.at[0])
    arrived(cols(gq_ref, other, QW), out_sem.at[1])
    for cp, cond in waits:
        if cond is None:
            cp.wait_send()
        else:
            @pl.when(cond)
            def _():
                cp.wait_send()


def body(n_ctx, n_tp, queries, key_rows, values, grad_out, lengths, pair_swap):
    bf, f32 = jnp.bfloat16, jnp.float32
    nd = REACH + 1
    kv_piece = pltpu.VMEM((2, BLK, HD), bf)
    any_spec = pl.BlockSpec(memory_space=pl.ANY)
    vmem_spec = pl.BlockSpec(memory_space=pltpu.VMEM)
    dma = pltpu.SemaphoreType.DMA
    return pl.pallas_call(
        functools.partial(kernel, n_ctx, n_tp),
        out_shape=(
            jax.ShapeDtypeStruct((1, BLK // n_tp, n_tp * 2 * QW), bf),
            jax.ShapeDtypeStruct(queries.shape, bf),
            jax.ShapeDtypeStruct(key_rows.shape, bf),
            jax.ShapeDtypeStruct(values.shape, bf),
        ),
        in_specs=[any_spec] * 4 + [pl.BlockSpec(memory_space=pltpu.SMEM), any_spec],
        out_specs=(any_spec, any_spec, vmem_spec, vmem_spec),
        scratch_shapes=[kv_piece] * 10 + [
            pltpu.VMEM((2, BLK, QW), bf),
            pltpu.VMEM((2, BLK, QW), bf),
            pltpu.SMEM((nd, 1), jnp.int32),
            pltpu.VMEM((2, nd, BLK, HD), bf),
            pltpu.VMEM((2, nd, BLK, HD), bf),
            pltpu.VMEM((2, QL, HD), bf),
            pltpu.VMEM((2, QL, HD), bf),
            pltpu.VMEM((2, nd, BLK, QL), f32),
            pltpu.VMEM((2, nd, BLK, QL), f32),
            pltpu.VMEM((2, nd, BLK, QL), bf),
            pltpu.VMEM((2, nd, BLK, QL), bf),
            pltpu.VMEM((2, BLK, QW), bf),
            pltpu.VMEM((2, BLK, QW), bf),
            pltpu.VMEM((nd, 2, 2, BLK, HD), bf),
            pltpu.VMEM((2, 2, BLK, HD), f32),
            pltpu.VMEM((2, BLK, HD), f32),
            pltpu.VMEM((3, 2, 2, BLK, HD), bf),
            pltpu.VMEM((2, 2, BLK, HD), bf),
            pltpu.VMEM((2, 2, BLK, HD), f32),
            pltpu.VMEM((3, 2, 2, BLK, HD), bf),
            dma((7,)),
            dma((64,)),
            dma((nd,)),
            dma((nd,)),
            dma((2,)),
            dma((nd,)),
            dma((2,)),
            dma((nd,)),
            dma((NX,)),
        ],
        compiler_params=pltpu.CompilerParams(collective_id=0, has_side_effects=True),
        name="attend",
    )(queries, key_rows, values, grad_out, lengths, pair_swap)


def solution(mesh):
    placed = P("dp", "ctx", "tp")
    return jax.shard_map(
        functools.partial(body, mesh.shape["ctx"], mesh.shape["tp"]),
        mesh=mesh,
        in_specs=(placed, placed, placed, placed, P(), P("ctx")),
        out_specs=(P("dp", ("ctx", "tp"), None), placed, placed, placed),
        check_vma=False,
    )
```

```python
import functools

import jax
import jax.numpy as jnp
from jax import lax
from jax.experimental import pallas as pl
from jax.experimental.pallas import tpu as pltpu
from jax.sharding import PartitionSpec as P

HD = 128
REP = 2
W = 512
BLK = 128
REACH = W // BLK
NX = 4
QW = REP * HD
QL = REP * BLK

SCALE = 168.0 ** (-0.5)
NEGATIVE = -1e30
MESH = pl.DeviceIdType.MESH
NT = (((1,), (1,)), ((), ()))
TN = (((0,), (0,)), ((), ()))
NN = (((1,), (0,)), ((), ()))


def mm(a, b, dims):
    return lax.dot_general(a, b, dims, preferred_element_type=jnp.float32)


def kernel(
    n_ctx, n_tp,
    q_ref, k_ref, v_ref, g_ref, len_ref, swap_ref,
    ao_ref, gq_ref, gk_ref, gv_ref,
    kb0, kb1, kb2, kb3, kb4, vb0, vb1, vb2, vb3, vb4, qb, gb, flags,
    ks, vs, qs, gs, sc, dp, pb, dsb,
    ob, dqb, part, own, mate, near, far, hub, relay,
    loc_sem, send_sem, rk_sem, rv_sem, rq_sem, rf_sem, out_sem, pd_sem, hub_sem,
):
    kb = (kb0, kb1, kb2, kb3, kb4)
    vb = (vb0, vb1, vb2, vb3, vb4)
    p = lax.axis_index("dp")
    c = lax.axis_index("ctx")
    y = lax.axis_index("tp")
    other = 1 - p
    x = lax.rem(c, NX)
    ahead = lax.rem(c + NX, n_ctx)
    behind = lax.rem(c + n_ctx - NX, n_ctx)

    first = c < NX
    final = c + NX >= n_ctx

    def cols(ref, j, width):
        return ref.at[0, :, pl.ds(pl.multiple_of(j * width, width), width)]

    local = [
        pltpu.make_async_copy(cols(k_ref, p, HD), kb0.at[p], loc_sem.at[0]),
        pltpu.make_async_copy(cols(q_ref, p, QW), qb.at[p], loc_sem.at[1]),
        pltpu.make_async_copy(cols(v_ref, p, HD), vb0.at[p], loc_sem.at[2]),
        pltpu.make_async_copy(cols(g_ref, p, QW), gb.at[p], loc_sem.at[3]),
    ]
    for cp in local:
        cp.start()

    barrier = pltpu.get_barrier_semaphore()

    def greet(dev):
        pl.semaphore_signal(barrier, inc=1, device_id=dev, device_id_type=MESH)

    greet((other, c, y))
    met = 1
    for d in range(1, NX):
        for j in range(2):
            greet((j, c - x + lax.rem(x + d, NX), y))
            met += 1
    for d in range(1, n_tp):
        for j in range(2):
            greet((j, c, lax.rem(y + d, n_tp)))
            met += 1

    @pl.when(jnp.logical_not(final))
    def _():
        for j in range(2):
            greet((j, ahead, y))

    @pl.when(jnp.logical_not(first))
    def _():
        for j in range(2):
            greet((j, behind, y))

    pl.semaphore_wait(barrier, met + 2 * (1 - first.astype(jnp.int32)) + 2 * (1 - final.astype(jnp.int32)))

    count = [0]
    waits = []

    def remote(src, dst, recv, dev, cond=None):
        sem = send_sem.at[count[0]]
        count[0] += 1
        cp = pltpu.make_async_remote_copy(
            src_ref=src, dst_ref=dst, send_sem=sem, recv_sem=recv,
            device_id=dev, device_id_type=MESH,
        )
        if cond is None:
            cp.start()
        else:
            @pl.when(cond)
            def _():
                cp.start()
        waits.append((cp, cond))
        return cp

    def arrived(ref, sem, cond=None):
        if cond is None:
            pltpu.make_async_copy(ref, ref, sem).wait()
        else:
            @pl.when(cond)
            def _():
                pltpu.make_async_copy(ref, ref, sem).wait()

    mine = (other, c, y)
    inner = jnp.logical_not(first)
    onward = jnp.logical_not(final)
    for j in range(2):
        remote(cols(k_ref, j, HD), kb4.at[p], rk_sem.at[4], (j, ahead, y), onward)
    remote(cols(k_ref, other, HD), kb0.at[p], rk_sem.at[0], mine)
    remote(cols(q_ref, other, QW), qb.at[p], rq_sem.at[0], mine)
    for d in (2, 1, 3):
        for j in range(2):
            remote(cols(k_ref, j, HD), kb[d].at[p], rk_sem.at[d], (j, lax.rem(c + d, n_ctx), y), x + d < NX)
    remote(cols(g_ref, other, QW), gb.at[p], rq_sem.at[1], mine)
    for j in range(2):
        remote(cols(v_ref, j, HD), vb4.at[p], rv_sem.at[4], (j, ahead, y), onward)
    remote(cols(v_ref, other, HD), vb0.at[p], rv_sem.at[0], mine)
    for d in (2, 1, 3):
        for j in range(2):
            remote(cols(v_ref, j, HD), vb[d].at[p], rv_sem.at[d], (j, lax.rem(c + d, n_ctx), y), x + d < NX)
    remote(swap_ref.at[0], flags.at[4], rf_sem.at[4], (p, ahead, y), onward)
    for d in range(1, NX):
        remote(swap_ref.at[0], flags.at[d], rf_sem.at[d], (p, lax.rem(c + d, n_ctx), y), x + d < NX)

    for d in range(1, REACH + 1):
        @pl.when(c < d)
        def _():
            flags[d, 0] = 0
            kb[d][...] = jnp.zeros_like(kb[d])
            vb[d][...] = jnp.zeros_like(vb[d])

    lane = lax.broadcasted_iota(jnp.int32, (1, BLK), 1)
    pos = c * BLK + lane
    lows = []
    for pi in range(2):
        low = jnp.maximum(pos - (W - 1), 0)
        end = jnp.int32(0)
        for r in range(len_ref.shape[1]):
            end = end + len_ref[pi, r]
            low = jnp.maximum(low, jnp.where(pos >= end, end, 0))
        lows.append(jnp.concatenate([low] * REP, axis=1) - c * BLK)
    lane2 = jnp.concatenate([lane] * REP, axis=1)
    row_id = lax.broadcasted_iota(jnp.int32, (BLK, QL), 0)

    def pick(ref, swapped, pi):
        a, b = ref[pi], ref[1 - pi]
        return jnp.where(swapped, b, a)

    def take(d):
        swapped = (swap_ref[0, 0] if d == 0 else flags[d, 0]) == 1
        for pi in range(2):
            key = pick(kb[d], swapped, pi)
            ks[pi, d] = key
            s = mm(key, qs[pi], NT) * SCALE
            ok = row_id - d * BLK >= lows[pi]
            if d == 0:
                ok = ok & (row_id <= lane2)
            sc[pi, d] = jnp.where(ok, s, NEGATIVE)

    def take_v(d):
        swapped = (swap_ref[0, 0] if d == 0 else flags[d, 0]) == 1
        for pi in range(2):
            val = pick(vb[d], swapped, pi)
            vs[pi, d] = val
            dp[pi, d] = mm(val, gs[pi], NT)

    def stack(src, dst, swapped):
        for pi in range(2):
            t = pick(src, swapped, pi)
            for r in range(REP):
                dst[pi, r * BLK:(r + 1) * BLK] = t[:, r * HD:(r + 1) * HD]

    for cp in local:
        cp.wait()
    swapped = swap_ref[0, 0] == 1
    arrived(qb.at[other], rq_sem.at[0])
    stack(qb, qs, swapped)
    arrived(kb0.at[other], rk_sem.at[0])
    take(0)
    arrived(gb.at[other], rq_sem.at[1])
    stack(gb, gs, swapped)

    def pass_on(buf, sem):
        arrived(buf[4], sem.at[4], inner)
        for e in (2, 1, 3):
            remote(buf[4], buf[4 - e], sem.at[4 - e], (p, lax.rem(c + n_ctx - e, n_ctx), y), inner & (x >= e))

    pass_on(kb, rk_sem)
    arrived(flags.at[4], rf_sem.at[4], inner)
    for e in range(1, NX):
        remote(flags.at[4], flags.at[4 - e], rf_sem.at[4 - e], (p, lax.rem(c + n_ctx - e, n_ctx), y), inner & (x >= e))
    take(4)
    pass_on(vb, rv_sem)
    arrived(vb0.at[other], rv_sem.at[0])
    take_v(0)
    take_v(4)
    for d in (1, 2, 3):
        arrived(flags.at[d], rf_sem.at[d], c >= d)
        arrived(kb[d], rk_sem.at[d], c >= d)
        take(d)

    def give(s, d):
        dev = lax.rem(c + n_ctx - d, n_ctx)
        for pi in range(2):
            remote(part.at[d, s, pi], near.at[d - 1, s, p], pd_sem.at[s, d], (pi, dev, y), x >= d)
        remote(part.at[d, s], relay.at[NX - d - 1, s], hub_sem.at[s, NX - d], (p, c + NX - d, y), inner & (x < d))

    for pi in range(2):
        top = jnp.max(sc[pi, 0], axis=0, keepdims=True)
        for d in range(1, REACH + 1):
            top = jnp.maximum(top, jnp.max(sc[pi, d], axis=0, keepdims=True))
        total = jnp.zeros((1, QL), jnp.float32)
        for d in range(REACH + 1):
            e = jnp.exp(sc[pi, d] - top)
            sc[pi, d] = e
            total = total + jnp.sum(e, axis=0, keepdims=True)
        inv = 1.0 / total
        for d in (3, 2, 1, 4, 0):
            pr = sc[pi, d] * inv
            sc[pi, d] = pr
            pb[pi, d] = pr.astype(jnp.bfloat16)
            dv = mm(pb[pi, d], gs[pi], NN)
            if d == 0:
                own[1, pi] = dv
            elif d == 4:
                hub[1, pi] = dv
            else:
                part[d, 1, pi] = dv.astype(jnp.bfloat16)
    for d in (3, 2, 1):
        give(1, d)
    remote(own.at[1, other], mate.at[1], pd_sem.at[1, 0], mine)

    for d in (1, 2, 3):
        arrived(vb[d], rv_sem.at[d], c >= d)
        take_v(d)
    for pi in range(2):
        delta = jnp.zeros((1, QL), jnp.float32)
        for d in range(REACH + 1):
            delta = delta + jnp.sum(sc[pi, d] * dp[pi, d], axis=0, keepdims=True)
        for d in (3, 2, 1, 4, 0):
            dsb[pi, d] = (sc[pi, d] * (dp[pi, d] - delta)).astype(jnp.bfloat16)
            dk = mm(dsb[pi, d], qs[pi], NN) * SCALE
            if d == 0:
                own[0, pi] = dk
            elif d == 4:
                hub[0, pi] = dk
            else:
                part[d, 0, pi] = dk.astype(jnp.bfloat16)
    for d in (3, 2, 1):
        give(0, d)
    remote(own.at[0, other], mate.at[0], pd_sem.at[0, 0], mine)

    for pi in range(2):
        o = mm(pb[pi].reshape(-1, QL), vs[pi].reshape(-1, HD), TN).astype(jnp.bfloat16)
        for r in range(REP):
            ob[pi, :, r * HD:(r + 1) * HD] = o[r * BLK:(r + 1) * BLK]
    share = BLK // n_tp
    width = REP * HD
    at = pl.ds(pl.multiple_of((y * 2 + p) * width, width), width)
    for dt in range(n_tp):
        t = lax.rem(y + dt, n_tp)
        rows = pl.ds(pl.multiple_of(t * share, share), share)
        for dj in range(2):
            pi = p if dj == 0 else other
            if dt == 0 and dj == 0:
                keep = pltpu.make_async_copy(ob.at[pi, rows], ao_ref.at[0, :, at], loc_sem.at[5])
                keep.start()
            else:
                remote(ob.at[pi, rows], ao_ref.at[0, :, at], out_sem.at[0], (pi, c, t))
    for pi in range(2):
        o = (mm(dsb[pi].reshape(-1, QL), ks[pi].reshape(-1, HD), TN) * SCALE).astype(jnp.bfloat16)
        for r in range(REP):
            dqb[pi, :, r * HD:(r + 1) * HD] = o[r * BLK:(r + 1) * BLK]
    keep_q = pltpu.make_async_copy(dqb.at[p], cols(gq_ref, p, QW), loc_sem.at[6])
    keep_q.start()
    remote(dqb.at[other], cols(gq_ref, p, QW), out_sem.at[1], mine)

    for s in (1, 0):
        for e in range(1, NX):
            @pl.when(inner & (x >= e))
            def _():
                arrived(relay.at[e - 1, s], hub_sem.at[s, e])
                for pi in range(2):
                    hub[s, pi] = hub[s, pi] + relay[e - 1, s, pi].astype(jnp.float32)
        for pi in range(2):
            part[4, s, pi] = hub[s, pi].astype(jnp.bfloat16)
        for pi in range(2):
            remote(part.at[4, s, pi], far.at[s, p], pd_sem.at[s, 4], (pi, behind, y), inner)

    for s, out in ((1, gv_ref), (0, gk_ref)):
        arrived(mate.at[s], pd_sem.at[s, 0])
        for d in range(1, NX):
            @pl.when(x + d < NX)
            def _():
                arrived(near.at[d - 1, s], pd_sem.at[s, d])
                own[s, p] = own[s, p] + near[d - 1, s, p].astype(jnp.float32)
                mate[s] = mate[s] + near[d - 1, s, other].astype(jnp.float32)

        @pl.when(onward)
        def _():
            arrived(far.at[s], pd_sem.at[s, 4])
            own[s, p] = own[s, p] + far[s, p].astype(jnp.float32)
            mate[s] = mate[s] + far[s, other].astype(jnp.float32)
        for j, src in ((p, own[s, p]), (other, mate[s])):
            out[0, :, pl.ds(pl.multiple_of(j * HD, HD), HD)] = src.astype(jnp.bfloat16)

    keep.wait()
    keep_q.wait()
    arrived(ao_ref.at[0, :, pl.ds(0, (2 * n_tp - 1) * width)], out_sem.at[0])
    arrived(cols(gq_ref, other, QW), out_sem.at[1])
    for cp, cond in waits:
        if cond is None:
            cp.wait_send()
        else:
            @pl.when(cond)
            def _():
                cp.wait_send()


def store(a_ref, b_ref, c_ref, d_ref, ao_ref, gq_ref, gk_ref, gv_ref, sem):
    copies = [
        pltpu.make_async_copy(src, dst, sem.at[i])
        for i, (src, dst) in enumerate(((a_ref, ao_ref), (b_ref, gq_ref), (c_ref, gk_ref), (d_ref, gv_ref)))
    ]
    for cp in copies:
        cp.start()
    for cp in copies:
        cp.wait()


def body(n_ctx, n_tp, queries, key_rows, values, grad_out, lengths, pair_swap):
    bf, f32 = jnp.bfloat16, jnp.float32
    nd = REACH + 1
    kv_piece = pltpu.VMEM((2, BLK, HD), bf)
    any_spec = pl.BlockSpec(memory_space=pl.ANY)
    vmem_spec = pl.BlockSpec(memory_space=pltpu.VMEM)
    dma = pltpu.SemaphoreType.DMA
    shapes = (
        ((1, BLK // n_tp, n_tp * 2 * QW), bf),
        (queries.shape, bf),
        (key_rows.shape, bf),
        (values.shape, bf),
    )
    held = pl.pallas_call(
        functools.partial(kernel, n_ctx, n_tp),
        out_shape=tuple(pltpu.VMEM(*item) for item in shapes),
        in_specs=[any_spec] * 4 + [pl.BlockSpec(memory_space=pltpu.SMEM)] * 2,
        out_specs=(vmem_spec,) * 4,
        scratch_shapes=[kv_piece] * 10 + [
            pltpu.VMEM((2, BLK, QW), bf),
            pltpu.VMEM((2, BLK, QW), bf),
            pltpu.SMEM((nd, 1), jnp.int32),
            pltpu.VMEM((2, nd, BLK, HD), bf),
            pltpu.VMEM((2, nd, BLK, HD), bf),
            pltpu.VMEM((2, QL, HD), bf),
            pltpu.VMEM((2, QL, HD), bf),
            pltpu.VMEM((2, nd, BLK, QL), f32),
            pltpu.VMEM((2, nd, BLK, QL), f32),
            pltpu.VMEM((2, nd, BLK, QL), bf),
            pltpu.VMEM((2, nd, BLK, QL), bf),
            pltpu.VMEM((2, BLK, QW), bf),
            pltpu.VMEM((2, BLK, QW), bf),
            pltpu.VMEM((nd, 2, 2, BLK, HD), bf),
            pltpu.VMEM((2, 2, BLK, HD), f32),
            pltpu.VMEM((2, BLK, HD), f32),
            pltpu.VMEM((3, 2, 2, BLK, HD), bf),
            pltpu.VMEM((2, 2, BLK, HD), bf),
            pltpu.VMEM((2, 2, BLK, HD), f32),
            pltpu.VMEM((3, 2, 2, BLK, HD), bf),
            dma((7,)),
            dma((80,)),
            dma((nd,)),
            dma((nd,)),
            dma((2,)),
            dma((nd,)),
            dma((2,)),
            dma((2, nd)),
            dma((2, NX)),
        ],
        compiler_params=pltpu.CompilerParams(collective_id=0, has_side_effects=True),
        name="attend",
    )(queries, key_rows, values, grad_out, lengths, pair_swap.reshape(1, 1))
    return pl.pallas_call(
        store,
        out_shape=tuple(jax.ShapeDtypeStruct(*item) for item in shapes),
        in_specs=[any_spec] * 4,
        out_specs=(any_spec,) * 4,
        scratch_shapes=[dma((4,))],
        name="store",
    )(*[pltpu.with_memory_space_constraint(item, pltpu.VMEM) for item in held])


def solution(mesh):
    placed = P("dp", "ctx", "tp")
    return jax.shard_map(
        functools.partial(body, mesh.shape["ctx"], mesh.shape["tp"]),
        mesh=mesh,
        in_specs=(placed, placed, placed, placed, P(), P("ctx")),
        out_specs=(P("dp", ("ctx", "tp"), None), placed, placed, placed),
        check_vma=False,
    )
```

```python
import functools

import jax
import jax.numpy as jnp
from jax import lax
from jax.experimental import pallas as pl
from jax.experimental.pallas import tpu as pltpu
from jax.sharding import PartitionSpec as P

HD = 128
REP = 2
W = 512
BLK = 128
REACH = W // BLK
NX = 4
QW = REP * HD
QL = REP * BLK

SCALE = 168.0 ** (-0.5)
NEGATIVE = -1e30
MESH = pl.DeviceIdType.MESH
NT = (((1,), (1,)), ((), ()))
TN = (((0,), (0,)), ((), ()))
NN = (((1,), (0,)), ((), ()))


def mm(a, b, dims):
    return lax.dot_general(a, b, dims, preferred_element_type=jnp.float32)


def kernel(
    n_ctx, n_tp,
    q_ref, k_ref, v_ref, g_ref, len_ref, swap_ref,
    ao_ref, gq_ref, gk_ref, gv_ref,
    kb0, kb1, kb2, kb3, kb4, vb0, vb1, vb2, vb3, vb4, qb, gb, flags,
    ks, vs, qs, gs, sc, dp, pb, dsb,
    ob, dqb, part, own, mate, near, far, hub, relay,
    loc_sem, late_sem, send_sem, rk_sem, rv_sem, rq_sem, rf_sem, out_sem, pd_sem, hub_sem,
):
    kb = (kb0, kb1, kb2, kb3, kb4)
    vb = (vb0, vb1, vb2, vb3, vb4)
    p = lax.axis_index("dp")
    c = lax.axis_index("ctx")
    y = lax.axis_index("tp")
    other = 1 - p
    x = lax.rem(c, NX)
    ahead = lax.rem(c + NX, n_ctx)
    behind = lax.rem(c + n_ctx - NX, n_ctx)

    first = c < NX
    final = c + NX >= n_ctx

    def cols(ref, j, width):
        return ref.at[0, :, pl.ds(pl.multiple_of(j * width, width), width)]

    local = [
        pltpu.make_async_copy(cols(k_ref, p, HD), kb0.at[p], loc_sem.at[0]),
        pltpu.make_async_copy(cols(q_ref, p, QW), qb.at[p], loc_sem.at[1]),
        pltpu.make_async_copy(cols(v_ref, p, HD), vb0.at[p], loc_sem.at[2]),
        pltpu.make_async_copy(cols(g_ref, p, QW), gb.at[p], loc_sem.at[3]),
    ]
    for cp in local:
        cp.start()

    barrier = pltpu.get_barrier_semaphore()

    def greet(dev):
        pl.semaphore_signal(barrier, inc=1, device_id=dev, device_id_type=MESH)

    inner = jnp.logical_not(first)
    onward = jnp.logical_not(final)
    skip_on = (x >= NX // 2) & onward
    skip_back = (x < NX // 2) & inner

    latest = (p == 0) & (c == 0) & (y == 0)
    by_latest = jnp.logical_not(latest) & (((y == 0) & (c <= NX)) | (c == 0))

    @pl.when(jnp.logical_not(latest))
    def _():
        greet((other, c, y))
        for j in range(2):
            for d in range(1, NX):
                greet((j, c - x + lax.rem(x + d, NX), y))
            for d in range(1, n_tp):
                greet((j, c, lax.rem(y + d, n_tp)))
        for cond, dev in (
            (onward, ahead),
            (inner, behind),
            (skip_on, lax.rem(c + 2, n_ctx)),
            (skip_back, lax.rem(c + n_ctx - 2, n_ctx)),
        ):
            @pl.when(cond)
            def _():
                for j in range(2):
                    greet((j, dev, y))

    met = 1 + 2 * (NX - 1) + 2 * (n_tp - 1) - by_latest.astype(jnp.int32)
    for cond in (onward, inner, skip_on, skip_back):
        met = met + 2 * cond.astype(jnp.int32)
    pl.semaphore_wait(barrier, met)

    @pl.when(latest)
    def _():
        beside = [(1, 0, 0)]
        for j in range(2):
            beside += [(j, d, 0) for d in range(1, min(NX + 1, n_ctx))]
            beside += [(j, 0, t) for t in range(1, n_tp)]
        for dev in beside:
            pl.semaphore_signal(late_sem, inc=1, device_id=dev, device_id_type=MESH)

    def meet_latest(cond):
        @pl.when(by_latest & cond)
        def _():
            pl.semaphore_wait(late_sem, 1)

    count = [0]
    waits = []

    def remote(src, dst, recv, dev, cond=None):
        sem = send_sem.at[count[0]]
        count[0] += 1
        cp = pltpu.make_async_remote_copy(
            src_ref=src, dst_ref=dst, send_sem=sem, recv_sem=recv,
            device_id=dev, device_id_type=MESH,
        )
        if cond is None:
            cp.start()
        else:
            @pl.when(cond)
            def _():
                cp.start()
        waits.append((cp, cond))
        return cp

    def arrived(ref, sem, cond=None):
        if cond is None:
            pltpu.make_async_copy(ref, ref, sem).wait()
        else:
            @pl.when(cond)
            def _():
                pltpu.make_async_copy(ref, ref, sem).wait()

    mine = (other, c, y)

    def later(d):
        return lax.rem(c + d, n_ctx)

    def earlier(d):
        return lax.rem(c + n_ctx - d, n_ctx)

    def reaches(d):
        return c + 2 < n_ctx if d == 2 else onward if d == REACH else x + d < NX

    for d in (4, 1, 3, 2):
        remote(swap_ref.at[0], flags.at[d], rf_sem.at[d], (p, later(d), y), reaches(d))
    for src, dst, sem, d in (
        (k_ref, kb, rk_sem, 4),
        (k_ref, kb, rk_sem, 1),
        (k_ref, kb, rk_sem, 3),
        (v_ref, vb, rv_sem, 4),
        (k_ref, kb, rk_sem, 2),
        (v_ref, vb, rv_sem, 1),
        (v_ref, vb, rv_sem, 3),
        (v_ref, vb, rv_sem, 2),
    ):
        for j in range(2):
            remote(cols(src, j, HD), dst[d].at[p], sem.at[d], (j, later(d), y), reaches(d))
    meet_latest((y == 0) & (c == 0))
    remote(cols(q_ref, other, QW), qb.at[p], rq_sem.at[0], mine)
    remote(cols(k_ref, other, HD), kb0.at[p], rk_sem.at[0], mine)
    remote(cols(g_ref, other, QW), gb.at[p], rq_sem.at[1], mine)
    remote(cols(v_ref, other, HD), vb0.at[p], rv_sem.at[0], mine)

    for d in range(1, REACH + 1):
        @pl.when(c < d)
        def _():
            flags[d, 0] = 0
            kb[d][...] = jnp.zeros_like(kb[d])
            vb[d][...] = jnp.zeros_like(vb[d])

    lane = lax.broadcasted_iota(jnp.int32, (1, BLK), 1)
    pos = c * BLK + lane
    lows = []
    for pi in range(2):
        low = jnp.maximum(pos - (W - 1), 0)
        end = jnp.int32(0)
        for r in range(len_ref.shape[1]):
            end = end + len_ref[pi, r]
            low = jnp.maximum(low, jnp.where(pos >= end, end, 0))
        lows.append(jnp.concatenate([low] * REP, axis=1) - c * BLK)
    lane2 = jnp.concatenate([lane] * REP, axis=1)
    row_id = lax.broadcasted_iota(jnp.int32, (BLK, QL), 0)

    def pick(ref, swapped, pi):
        a, b = ref[pi], ref[1 - pi]
        return jnp.where(swapped, b, a)

    def take(d):
        swapped = (swap_ref[0, 0] if d == 0 else flags[d, 0]) == 1
        for pi in range(2):
            key = pick(kb[d], swapped, pi)
            ks[pi, d] = key
            s = mm(key, qs[pi], NT) * SCALE
            ok = row_id - d * BLK >= lows[pi]
            if d == 0:
                ok = ok & (row_id <= lane2)
            sc[pi, d] = jnp.where(ok, s, NEGATIVE)

    def take_v(d):
        swapped = (swap_ref[0, 0] if d == 0 else flags[d, 0]) == 1
        for pi in range(2):
            val = pick(vb[d], swapped, pi)
            vs[pi, d] = val
            dp[pi, d] = mm(val, gs[pi], NT)

    def stack(src, dst, swapped):
        for pi in range(2):
            t = pick(src, swapped, pi)
            for r in range(REP):
                dst[pi, r * BLK:(r + 1) * BLK] = t[:, r * HD:(r + 1) * HD]

    for cp in local:
        cp.wait()
    swapped = swap_ref[0, 0] == 1
    arrived(qb.at[other], rq_sem.at[0])
    stack(qb, qs, swapped)
    arrived(kb0.at[other], rk_sem.at[0])
    take(0)
    arrived(gb.at[other], rq_sem.at[1])
    stack(gb, gs, swapped)

    def pass_on(src, dst, sem):
        arrived(src, sem.at[4], inner)
        for e in (1, 3):
            remote(src, dst(4 - e), sem.at[4 - e], (p, earlier(e), y), inner & (x >= e))

    pass_on(flags.at[4], lambda d: flags.at[d], rf_sem)
    pass_on(kb[4], lambda d: kb[d], rk_sem)
    take(4)
    pass_on(vb[4], lambda d: vb[d], rv_sem)
    arrived(vb0.at[other], rv_sem.at[0])
    take_v(0)
    take_v(4)
    for d in (2, 1, 3):
        arrived(flags.at[d], rf_sem.at[d], c >= d)
        arrived(kb[d], rk_sem.at[d], c >= d)
        take(d)

    def give(s, d):
        direct = c >= 2 if d == 2 else x >= d
        for pi in range(2):
            remote(part.at[d, s, pi], near.at[d - 1, s, p], pd_sem.at[s, d], (pi, earlier(d), y), direct)
        if d != 2:
            remote(part.at[d, s], relay.at[NX - d - 1, s], hub_sem.at[s, NX - d], (p, c + NX - d, y), inner & (x < d))

    for pi in range(2):
        top = jnp.max(sc[pi, 0], axis=0, keepdims=True)
        for d in range(1, REACH + 1):
            top = jnp.maximum(top, jnp.max(sc[pi, d], axis=0, keepdims=True))
        total = jnp.zeros((1, QL), jnp.float32)
        for d in range(REACH + 1):
            e = jnp.exp(sc[pi, d] - top)
            sc[pi, d] = e
            total = total + jnp.sum(e, axis=0, keepdims=True)
        inv = 1.0 / total
        for d in (3, 2, 1, 4, 0):
            pr = sc[pi, d] * inv
            sc[pi, d] = pr
            pb[pi, d] = pr.astype(jnp.bfloat16)
            dv = mm(pb[pi, d], gs[pi], NN)
            if d == 0:
                own[1, pi] = dv
            elif d == 4:
                hub[1, pi] = dv
            else:
                part[d, 1, pi] = dv.astype(jnp.bfloat16)
    meet_latest((y == 0) & (c > 0))
    for d in (3, 1, 2):
        give(1, d)
    remote(own.at[1, other], mate.at[1], pd_sem.at[1, 0], mine)

    for d in (2, 1, 3):
        arrived(vb[d], rv_sem.at[d], c >= d)
        take_v(d)
    for pi in range(2):
        delta = jnp.zeros((1, QL), jnp.float32)
        for d in range(REACH + 1):
            delta = delta + jnp.sum(sc[pi, d] * dp[pi, d], axis=0, keepdims=True)
        for d in (3, 2, 1, 4, 0):
            dsb[pi, d] = (sc[pi, d] * (dp[pi, d] - delta)).astype(jnp.bfloat16)
            dk = mm(dsb[pi, d], qs[pi], NN) * SCALE
            if d == 0:
                own[0, pi] = dk
            elif d == 4:
                hub[0, pi] = dk
            else:
                part[d, 0, pi] = dk.astype(jnp.bfloat16)
    for d in (3, 1, 2):
        give(0, d)
    remote(own.at[0, other], mate.at[0], pd_sem.at[0, 0], mine)

    for pi in range(2):
        o = (mm(dsb[pi].reshape(-1, QL), ks[pi].reshape(-1, HD), TN) * SCALE).astype(jnp.bfloat16)
        for r in range(REP):
            dqb[pi, :, r * HD:(r + 1) * HD] = o[r * BLK:(r + 1) * BLK]
    keep_q = pltpu.make_async_copy(dqb.at[p], cols(gq_ref, p, QW), loc_sem.at[6])
    keep_q.start()
    remote(dqb.at[other], cols(gq_ref, p, QW), out_sem.at[1], mine)
    for pi in range(2):
        o = mm(pb[pi].reshape(-1, QL), vs[pi].reshape(-1, HD), TN).astype(jnp.bfloat16)
        for r in range(REP):
            ob[pi, :, r * HD:(r + 1) * HD] = o[r * BLK:(r + 1) * BLK]
    meet_latest(y > 0)
    share = BLK // n_tp
    width = REP * HD
    at = pl.ds(pl.multiple_of((y * 2 + p) * width, width), width)
    for dt in range(n_tp):
        t = lax.rem(y + dt, n_tp)
        rows = pl.ds(pl.multiple_of(t * share, share), share)
        for dj in range(2):
            pi = p if dj == 0 else other
            if dt == 0 and dj == 0:
                keep = pltpu.make_async_copy(ob.at[pi, rows], ao_ref.at[0, :, at], loc_sem.at[5])
                keep.start()
            else:
                remote(ob.at[pi, rows], ao_ref.at[0, :, at], out_sem.at[0], (pi, c, t))

    for s in (1, 0):
        for e in (1, 3):
            @pl.when(inner & (x >= e))
            def _():
                arrived(relay.at[e - 1, s], hub_sem.at[s, e])
                for pi in range(2):
                    hub[s, pi] = hub[s, pi] + relay[e - 1, s, pi].astype(jnp.float32)
        for pi in range(2):
            part[4, s, pi] = hub[s, pi].astype(jnp.bfloat16)
        for pi in range(2):
            remote(part.at[4, s, pi], far.at[s, p], pd_sem.at[s, 4], (pi, behind, y), inner)

    for s, out in ((1, gv_ref), (0, gk_ref)):
        arrived(mate.at[s], pd_sem.at[s, 0])
        for d in range(1, NX):
            @pl.when(reaches(d))
            def _():
                arrived(near.at[d - 1, s], pd_sem.at[s, d])
                own[s, p] = own[s, p] + near[d - 1, s, p].astype(jnp.float32)
                mate[s] = mate[s] + near[d - 1, s, other].astype(jnp.float32)

        @pl.when(onward)
        def _():
            arrived(far.at[s], pd_sem.at[s, 4])
            own[s, p] = own[s, p] + far[s, p].astype(jnp.float32)
            mate[s] = mate[s] + far[s, other].astype(jnp.float32)
        for j, src in ((p, own[s, p]), (other, mate[s])):
            out[0, :, pl.ds(pl.multiple_of(j * HD, HD), HD)] = src.astype(jnp.bfloat16)

    keep.wait()
    keep_q.wait()
    arrived(ao_ref.at[0, :, pl.ds(0, (2 * n_tp - 1) * width)], out_sem.at[0])
    arrived(cols(gq_ref, other, QW), out_sem.at[1])
    for cp, cond in waits:
        if cond is None:
            cp.wait_send()
        else:
            @pl.when(cond)
            def _():
                cp.wait_send()


def store(a_ref, b_ref, c_ref, d_ref, ao_ref, gq_ref, gk_ref, gv_ref, sem):
    copies = [
        pltpu.make_async_copy(src, dst, sem.at[i])
        for i, (src, dst) in enumerate(((a_ref, ao_ref), (b_ref, gq_ref), (c_ref, gk_ref), (d_ref, gv_ref)))
    ]
    for cp in copies:
        cp.start()
    for cp in copies:
        cp.wait()


def body(n_ctx, n_tp, queries, key_rows, values, grad_out, lengths, pair_swap):
    bf, f32 = jnp.bfloat16, jnp.float32
    nd = REACH + 1
    kv_piece = pltpu.VMEM((2, BLK, HD), bf)
    any_spec = pl.BlockSpec(memory_space=pl.ANY)
    vmem_spec = pl.BlockSpec(memory_space=pltpu.VMEM)
    dma = pltpu.SemaphoreType.DMA
    shapes = (
        ((1, BLK // n_tp, n_tp * 2 * QW), bf),
        (queries.shape, bf),
        (key_rows.shape, bf),
        (values.shape, bf),
    )
    held = pl.pallas_call(
        functools.partial(kernel, n_ctx, n_tp),
        out_shape=tuple(pltpu.VMEM(*item) for item in shapes),
        in_specs=[any_spec] * 4 + [pl.BlockSpec(memory_space=pltpu.SMEM)] * 2,
        out_specs=(vmem_spec,) * 4,
        scratch_shapes=[kv_piece] * 10 + [
            pltpu.VMEM((2, BLK, QW), bf),
            pltpu.VMEM((2, BLK, QW), bf),
            pltpu.SMEM((nd, 1), jnp.int32),
            pltpu.VMEM((2, nd, BLK, HD), bf),
            pltpu.VMEM((2, nd, BLK, HD), bf),
            pltpu.VMEM((2, QL, HD), bf),
            pltpu.VMEM((2, QL, HD), bf),
            pltpu.VMEM((2, nd, BLK, QL), f32),
            pltpu.VMEM((2, nd, BLK, QL), f32),
            pltpu.VMEM((2, nd, BLK, QL), bf),
            pltpu.VMEM((2, nd, BLK, QL), bf),
            pltpu.VMEM((2, BLK, QW), bf),
            pltpu.VMEM((2, BLK, QW), bf),
            pltpu.VMEM((nd, 2, 2, BLK, HD), bf),
            pltpu.VMEM((2, 2, BLK, HD), f32),
            pltpu.VMEM((2, BLK, HD), f32),
            pltpu.VMEM((3, 2, 2, BLK, HD), bf),
            pltpu.VMEM((2, 2, BLK, HD), bf),
            pltpu.VMEM((2, 2, BLK, HD), f32),
            pltpu.VMEM((3, 2, 2, BLK, HD), bf),
            dma((7,)),
            pltpu.SemaphoreType.REGULAR,
            dma((80,)),
            dma((nd,)),
            dma((nd,)),
            dma((2,)),
            dma((nd,)),
            dma((2,)),
            dma((2, nd)),
            dma((2, NX)),
        ],
        compiler_params=pltpu.CompilerParams(collective_id=0, has_side_effects=True),
        name="attend",
    )(queries, key_rows, values, grad_out, lengths, pair_swap.reshape(1, 1))
    return pl.pallas_call(
        store,
        out_shape=tuple(jax.ShapeDtypeStruct(*item) for item in shapes),
        in_specs=[any_spec] * 4,
        out_specs=(any_spec,) * 4,
        scratch_shapes=[dma((4,))],
        name="store",
    )(*[pltpu.with_memory_space_constraint(item, pltpu.VMEM) for item in held])


def solution(mesh):
    placed = P("dp", "ctx", "tp")
    return jax.shard_map(
        functools.partial(body, mesh.shape["ctx"], mesh.shape["tp"]),
        mesh=mesh,
        in_specs=(placed, placed, placed, placed, P(), P("ctx")),
        out_specs=(P("dp", ("ctx", "tp"), None), placed, placed, placed),
        check_vma=False,
    )
```

```python
import functools

import jax
import jax.numpy as jnp
from jax import lax
from jax.experimental import pallas as pl
from jax.experimental.pallas import tpu as pltpu
from jax.sharding import PartitionSpec as P

HD = 128
REP = 2
W = 512
BLK = 128
REACH = W // BLK
NX = 4
QW = REP * HD
QL = REP * BLK

SCALE = 168.0 ** (-0.5)
NEGATIVE = -1e30
MESH = pl.DeviceIdType.MESH
NT = (((1,), (1,)), ((), ()))
TN = (((0,), (0,)), ((), ()))
NN = (((1,), (0,)), ((), ()))


def mm(a, b, dims):
    return lax.dot_general(a, b, dims, preferred_element_type=jnp.float32)


def kernel(
    n_ctx, n_tp,
    q_ref, k_ref, v_ref, g_ref, len_ref, swap_ref,
    ao_ref, gq_ref, gk_ref, gv_ref,
    kb0, kb1, kb2, kb3, kb4, vb0, vb1, vb2, vb3, vb4, qb, gb, flags,
    ks, vs, qs, gs, sc, dp, pb, dsb,
    ob, dqb, part, own, mate, near, far, hub, relay,
    loc_sem, rk4_sem, rv4_sem, late_sem, send_sem, rk_sem, rv_sem, rq_sem, rf_sem, out_sem, pd_sem, hub_sem,
):
    kb = (kb0, kb1, kb2, kb3, kb4)
    vb = (vb0, vb1, vb2, vb3, vb4)
    p = lax.axis_index("dp")
    c = lax.axis_index("ctx")
    y = lax.axis_index("tp")
    other = 1 - p
    x = lax.rem(c, NX)
    ahead = lax.rem(c + NX, n_ctx)
    behind = lax.rem(c + n_ctx - NX, n_ctx)

    first = c < NX
    final = c + NX >= n_ctx

    def cols(ref, j, width):
        return ref.at[0, :, pl.ds(pl.multiple_of(j * width, width), width)]

    local = [
        pltpu.make_async_copy(cols(k_ref, p, HD), kb0.at[p], loc_sem.at[0]),
        pltpu.make_async_copy(cols(q_ref, p, QW), qb.at[p], loc_sem.at[1]),
        pltpu.make_async_copy(cols(v_ref, p, HD), vb0.at[p], loc_sem.at[2]),
        pltpu.make_async_copy(cols(g_ref, p, QW), gb.at[p], loc_sem.at[3]),
    ]
    for cp in local:
        cp.start()
    flags[0, 0] = swap_ref[0, 0]

    barrier = pltpu.get_barrier_semaphore()

    def greet(dev):
        pl.semaphore_signal(barrier, inc=1, device_id=dev, device_id_type=MESH)

    inner = jnp.logical_not(first)
    onward = jnp.logical_not(final)
    skip_on = (x >= NX // 2) & onward
    skip_back = (x < NX // 2) & inner

    latest = (p == 0) & (c == 0) & (y == 0)
    by_latest = jnp.logical_not(latest) & (((y == 0) & (c <= NX)) | (c == 0))

    @pl.when(jnp.logical_not(latest))
    def _():
        greet((other, c, y))
        for j in range(2):
            for d in range(1, NX):
                greet((j, c - x + lax.rem(x + d, NX), y))
            for d in range(1, n_tp):
                greet((j, c, lax.rem(y + d, n_tp)))
        for cond, dev in (
            (onward, ahead),
            (inner, behind),
            (skip_on, lax.rem(c + 2, n_ctx)),
            (skip_back, lax.rem(c + n_ctx - 2, n_ctx)),
        ):
            @pl.when(cond)
            def _():
                for j in range(2):
                    greet((j, dev, y))

    met = 1 + 2 * (NX - 1) + 2 * (n_tp - 1) - by_latest.astype(jnp.int32)
    for cond in (onward, inner, skip_on, skip_back):
        met = met + 2 * cond.astype(jnp.int32)
    pl.semaphore_wait(barrier, met)

    @pl.when(latest)
    def _():
        beside = [(1, 0, 0)]
        for j in range(2):
            beside += [(j, d, 0) for d in range(1, min(NX + 1, n_ctx))]
            beside += [(j, 0, t) for t in range(1, n_tp)]
        for dev in beside:
            pl.semaphore_signal(late_sem, inc=1, device_id=dev, device_id_type=MESH)

    def meet_latest(cond):
        @pl.when(by_latest & cond)
        def _():
            pl.semaphore_wait(late_sem, 1)

    count = [0]
    waits = []

    def remote(src, dst, recv, dev, cond=None):
        sem = send_sem.at[count[0]]
        count[0] += 1
        cp = pltpu.make_async_remote_copy(
            src_ref=src, dst_ref=dst, send_sem=sem, recv_sem=recv,
            device_id=dev, device_id_type=MESH,
        )
        if cond is None:
            cp.start()
        else:
            @pl.when(cond)
            def _():
                cp.start()
        waits.append((cp, cond))
        return cp

    def arrived(ref, sem, cond=None):
        if cond is None:
            pltpu.make_async_copy(ref, ref, sem).wait()
        else:
            @pl.when(cond)
            def _():
                pltpu.make_async_copy(ref, ref, sem).wait()

    mine = (other, c, y)

    def later(d):
        return lax.rem(c + d, n_ctx)

    def earlier(d):
        return lax.rem(c + n_ctx - d, n_ctx)

    def reaches(d):
        return c + 2 < n_ctx if d == 2 else onward if d == REACH else x + d < NX

    for d in (4, 1, 3, 2):
        remote(flags.at[0], flags.at[d], rf_sem.at[d], (p, later(d), y), reaches(d))
    def send(pieces):
        for src, dst, sem, d in pieces:
            for j in range(2):
                remote(cols(src, j, HD), dst[d].at[p], sem.at[d], (j, later(d), y), reaches(d))

    def send_half(src, dst, sem, h):
        rows = pl.ds(h * (BLK // 2), BLK // 2)
        for j in range(2):
            remote(
                src.at[0, rows, pl.ds(j * HD, HD)], dst.at[p, rows], sem.at[h], (j, ahead, y), onward,
            )

    send_half(k_ref, kb4, rk4_sem, 0)
    send_half(k_ref, kb4, rk4_sem, 1)
    send([(k_ref, kb, rk_sem, 1), (k_ref, kb, rk_sem, 3)])
    send_half(v_ref, vb4, rv4_sem, 0)
    send_half(v_ref, vb4, rv4_sem, 1)
    send([(k_ref, kb, rk_sem, 2), (v_ref, vb, rv_sem, 1), (v_ref, vb, rv_sem, 3), (v_ref, vb, rv_sem, 2)])
    meet_latest((y == 0) & (c == 0))
    remote(cols(q_ref, other, QW), qb.at[p], rq_sem.at[0], mine)
    remote(cols(k_ref, other, HD), kb0.at[p], rk_sem.at[0], mine)
    remote(cols(g_ref, other, QW), gb.at[p], rq_sem.at[1], mine)
    remote(cols(v_ref, other, HD), vb0.at[p], rv_sem.at[0], mine)

    for d in range(1, REACH + 1):
        @pl.when(c < d)
        def _():
            flags[d, 0] = 0
            kb[d][...] = jnp.zeros_like(kb[d])
            vb[d][...] = jnp.zeros_like(vb[d])

    lane = lax.broadcasted_iota(jnp.int32, (1, BLK), 1)
    pos = c * BLK + lane
    lows = []
    for pi in range(2):
        low = jnp.maximum(pos - (W - 1), 0)
        end = jnp.int32(0)
        for r in range(len_ref.shape[1]):
            end = end + len_ref[pi, r]
            low = jnp.maximum(low, jnp.where(pos >= end, end, 0))
        lows.append(jnp.concatenate([low] * REP, axis=1) - c * BLK)
    lane2 = jnp.concatenate([lane] * REP, axis=1)
    row_id = lax.broadcasted_iota(jnp.int32, (BLK, QL), 0)

    def pick(ref, swapped, pi):
        a, b = ref[pi], ref[1 - pi]
        return jnp.where(swapped, b, a)

    def take(d):
        swapped = (swap_ref[0, 0] if d == 0 else flags[d, 0]) == 1
        for pi in range(2):
            key = pick(kb[d], swapped, pi)
            ks[pi, d] = key
            s = mm(key, qs[pi], NT) * SCALE
            ok = row_id - d * BLK >= lows[pi]
            if d == 0:
                ok = ok & (row_id <= lane2)
            sc[pi, d] = jnp.where(ok, s, NEGATIVE)

    def take_v(d):
        swapped = (swap_ref[0, 0] if d == 0 else flags[d, 0]) == 1
        for pi in range(2):
            val = pick(vb[d], swapped, pi)
            vs[pi, d] = val
            dp[pi, d] = mm(val, gs[pi], NT)

    def stack(src, dst, swapped):
        for pi in range(2):
            t = pick(src, swapped, pi)
            for r in range(REP):
                dst[pi, r * BLK:(r + 1) * BLK] = t[:, r * HD:(r + 1) * HD]

    for cp in local:
        cp.wait()
    swapped = swap_ref[0, 0] == 1
    arrived(qb.at[other], rq_sem.at[0])
    stack(qb, qs, swapped)
    arrived(kb0.at[other], rk_sem.at[0])
    take(0)
    arrived(gb.at[other], rq_sem.at[1])
    stack(gb, gs, swapped)

    def pass_on(src, dst, sem):
        arrived(src, sem.at[4], inner)
        for e in (1, 3):
            remote(src, dst(4 - e), sem.at[4 - e], (p, earlier(e), y), inner & (x >= e))

    def pass_halves(buf, sem, own_sem):
        for h in range(2):
            rows = pl.ds(h * (BLK // 2), BLK // 2)
            arrived(buf[4].at[:, rows], own_sem.at[h], inner)
            for e in (1, 3):
                remote(
                    buf[4].at[:, rows], buf[4 - e].at[:, rows], sem.at[4 - e],
                    (p, earlier(e), y), inner & (x >= e),
                )

    pass_on(flags.at[4], lambda d: flags.at[d], rf_sem)
    pass_halves(kb, rk_sem, rk4_sem)
    take(4)
    pass_halves(vb, rv_sem, rv4_sem)
    arrived(vb0.at[other], rv_sem.at[0])
    take_v(0)
    take_v(4)
    for d in (2, 1, 3):
        arrived(flags.at[d], rf_sem.at[d], c >= d)
        arrived(kb[d], rk_sem.at[d], c >= d)
        take(d)

    def give(s, d, pi):
        direct = c >= 2 if d == 2 else x >= d
        remote(part.at[d, s, pi], near.at[d - 1, s, p], pd_sem.at[s, d], (pi, earlier(d), y), direct)
        if d != 2:
            remote(
                part.at[d, s, pi], relay.at[NX - d - 1, s, pi], hub_sem.at[s, pi, NX - d],
                (p, c + NX - d, y), inner & (x < d),
            )

    meet_latest((y == 0) & (c > 0))
    for pi in range(2):
        top = jnp.max(sc[pi, 0], axis=0, keepdims=True)
        for d in range(1, REACH + 1):
            top = jnp.maximum(top, jnp.max(sc[pi, d], axis=0, keepdims=True))
        total = jnp.zeros((1, QL), jnp.float32)
        for d in range(REACH + 1):
            e = jnp.exp(sc[pi, d] - top)
            sc[pi, d] = e
            total = total + jnp.sum(e, axis=0, keepdims=True)
        inv = 1.0 / total
        for d in (3, 1, 2, 4, 0):
            pr = sc[pi, d] * inv
            sc[pi, d] = pr
            pb[pi, d] = pr.astype(jnp.bfloat16)
            dv = mm(pb[pi, d], gs[pi], NN)
            if d == 0:
                own[1, pi] = dv
            elif d == 4:
                hub[1, pi] = dv
            else:
                part[d, 1, pi] = dv.astype(jnp.bfloat16)
        for d in (3, 1):
            give(1, d, pi)
    for pi in range(2):
        give(1, 2, pi)
    remote(own.at[1, other], mate.at[1], pd_sem.at[1, 0], mine)

    for d in (2, 1, 3):
        arrived(vb[d], rv_sem.at[d], c >= d)
        take_v(d)
    for pi in range(2):
        delta = jnp.zeros((1, QL), jnp.float32)
        for d in range(REACH + 1):
            delta = delta + jnp.sum(sc[pi, d] * dp[pi, d], axis=0, keepdims=True)
        for d in (3, 1, 2, 4, 0):
            dsb[pi, d] = (sc[pi, d] * (dp[pi, d] - delta)).astype(jnp.bfloat16)
            dk = mm(dsb[pi, d], qs[pi], NN) * SCALE
            if d == 0:
                own[0, pi] = dk
            elif d == 4:
                hub[0, pi] = dk
            else:
                part[d, 0, pi] = dk.astype(jnp.bfloat16)
        for d in (3, 1):
            give(0, d, pi)
    for pi in range(2):
        give(0, 2, pi)
    remote(own.at[0, other], mate.at[0], pd_sem.at[0, 0], mine)

    for pi in range(2):
        o = (mm(dsb[pi].reshape(-1, QL), ks[pi].reshape(-1, HD), TN) * SCALE).astype(jnp.bfloat16)
        for r in range(REP):
            dqb[pi, :, r * HD:(r + 1) * HD] = o[r * BLK:(r + 1) * BLK]
    keep_q = pltpu.make_async_copy(dqb.at[p], cols(gq_ref, p, QW), loc_sem.at[6])
    keep_q.start()
    remote(dqb.at[other], cols(gq_ref, p, QW), out_sem.at[1], mine)
    for pi in range(2):
        o = mm(pb[pi].reshape(-1, QL), vs[pi].reshape(-1, HD), TN).astype(jnp.bfloat16)
        for r in range(REP):
            ob[pi, :, r * HD:(r + 1) * HD] = o[r * BLK:(r + 1) * BLK]
    meet_latest(y > 0)
    share = BLK // n_tp
    width = REP * HD
    at = pl.ds(pl.multiple_of((y * 2 + p) * width, width), width)
    for dt in range(n_tp):
        t = lax.rem(y + dt, n_tp)
        rows = pl.ds(pl.multiple_of(t * share, share), share)
        for dj in range(2):
            pi = p if dj == 0 else other
            if dt == 0 and dj == 0:
                keep = pltpu.make_async_copy(ob.at[pi, rows], ao_ref.at[0, :, at], loc_sem.at[5])
                keep.start()
            else:
                remote(ob.at[pi, rows], ao_ref.at[0, :, at], out_sem.at[0], (pi, c, t))

    for s in (1, 0):
        for pi in range(2):
            for e in (1, 3):
                @pl.when(inner & (x >= e))
                def _():
                    arrived(relay.at[e - 1, s, pi], hub_sem.at[s, pi, e])
                    hub[s, pi] = hub[s, pi] + relay[e - 1, s, pi].astype(jnp.float32)
            part[4, s, pi] = hub[s, pi].astype(jnp.bfloat16)
            remote(part.at[4, s, pi], far.at[s, p], pd_sem.at[s, 4], (pi, behind, y), inner)

    for s, out in ((1, gv_ref), (0, gk_ref)):
        arrived(mate.at[s], pd_sem.at[s, 0])
        for d in range(1, NX):
            @pl.when(reaches(d))
            def _():
                arrived(near.at[d - 1, s], pd_sem.at[s, d])
                own[s, p] = own[s, p] + near[d - 1, s, p].astype(jnp.float32)
                mate[s] = mate[s] + near[d - 1, s, other].astype(jnp.float32)

        @pl.when(onward)
        def _():
            arrived(far.at[s], pd_sem.at[s, 4])
            own[s, p] = own[s, p] + far[s, p].astype(jnp.float32)
            mate[s] = mate[s] + far[s, other].astype(jnp.float32)
        for j, src in ((p, own[s, p]), (other, mate[s])):
            out[0, :, pl.ds(pl.multiple_of(j * HD, HD), HD)] = src.astype(jnp.bfloat16)

    keep.wait()
    keep_q.wait()
    arrived(ao_ref.at[0, :, pl.ds(0, (2 * n_tp - 1) * width)], out_sem.at[0])
    arrived(cols(gq_ref, other, QW), out_sem.at[1])
    for cp, cond in waits:
        if cond is None:
            cp.wait_send()
        else:
            @pl.when(cond)
            def _():
                cp.wait_send()


def store(a_ref, b_ref, c_ref, d_ref, ao_ref, gq_ref, gk_ref, gv_ref, sem):
    copies = [
        pltpu.make_async_copy(src, dst, sem.at[i])
        for i, (src, dst) in enumerate(((a_ref, ao_ref), (b_ref, gq_ref), (c_ref, gk_ref), (d_ref, gv_ref)))
    ]
    for cp in copies:
        cp.start()
    for cp in copies:
        cp.wait()


def body(n_ctx, n_tp, queries, key_rows, values, grad_out, lengths, pair_swap):
    bf, f32 = jnp.bfloat16, jnp.float32
    nd = REACH + 1
    kv_piece = pltpu.VMEM((2, BLK, HD), bf)
    any_spec = pl.BlockSpec(memory_space=pl.ANY)
    vmem_spec = pl.BlockSpec(memory_space=pltpu.VMEM)
    dma = pltpu.SemaphoreType.DMA
    shapes = (
        ((1, BLK // n_tp, n_tp * 2 * QW), bf),
        (queries.shape, bf),
        (key_rows.shape, bf),
        (values.shape, bf),
    )
    held = pl.pallas_call(
        functools.partial(kernel, n_ctx, n_tp),
        out_shape=tuple(pltpu.VMEM(*item) for item in shapes),
        in_specs=[any_spec] * 4 + [pl.BlockSpec(memory_space=pltpu.SMEM)] * 2,
        out_specs=(vmem_spec,) * 4,
        scratch_shapes=[kv_piece] * 10 + [
            pltpu.VMEM((2, BLK, QW), bf),
            pltpu.VMEM((2, BLK, QW), bf),
            pltpu.SMEM((nd, 1), jnp.int32),
            pltpu.VMEM((2, nd, BLK, HD), bf),
            pltpu.VMEM((2, nd, BLK, HD), bf),
            pltpu.VMEM((2, QL, HD), bf),
            pltpu.VMEM((2, QL, HD), bf),
            pltpu.VMEM((2, nd, BLK, QL), f32),
            pltpu.VMEM((2, nd, BLK, QL), f32),
            pltpu.VMEM((2, nd, BLK, QL), bf),
            pltpu.VMEM((2, nd, BLK, QL), bf),
            pltpu.VMEM((2, BLK, QW), bf),
            pltpu.VMEM((2, BLK, QW), bf),
            pltpu.VMEM((nd, 2, 2, BLK, HD), bf),
            pltpu.VMEM((2, 2, BLK, HD), f32),
            pltpu.VMEM((2, BLK, HD), f32),
            pltpu.VMEM((3, 2, 2, BLK, HD), bf),
            pltpu.VMEM((2, 2, BLK, HD), bf),
            pltpu.VMEM((2, 2, BLK, HD), f32),
            pltpu.VMEM((3, 2, 2, BLK, HD), bf),
            dma((7,)),
            dma((2,)),
            dma((2,)),
            pltpu.SemaphoreType.REGULAR,
            dma((100,)),
            dma((nd,)),
            dma((nd,)),
            dma((2,)),
            dma((nd,)),
            dma((2,)),
            dma((2, nd)),
            dma((2, 2, NX)),
        ],
        compiler_params=pltpu.CompilerParams(collective_id=0, has_side_effects=True),
        name="attend",
    )(queries, key_rows, values, grad_out, lengths, pair_swap.reshape(1, 1))
    return pl.pallas_call(
        store,
        out_shape=tuple(jax.ShapeDtypeStruct(*item) for item in shapes),
        in_specs=[any_spec] * 4,
        out_specs=(any_spec,) * 4,
        scratch_shapes=[dma((4,))],
        name="store",
    )(*[pltpu.with_memory_space_constraint(item, pltpu.VMEM) for item in held])


def solution(mesh):
    placed = P("dp", "ctx", "tp")
    return jax.shard_map(
        functools.partial(body, mesh.shape["ctx"], mesh.shape["tp"]),
        mesh=mesh,
        in_specs=(placed, placed, placed, placed, P(), P("ctx")),
        out_specs=(P("dp", ("ctx", "tp"), None), placed, placed, placed),
        check_vma=False,
    )
```

```python
import functools

import jax
import jax.numpy as jnp
from jax import lax
from jax.experimental import pallas as pl
from jax.experimental.pallas import tpu as pltpu
from jax.sharding import PartitionSpec as P

HD = 128
REP = 2
W = 512
BLK = 128
REACH = W // BLK
NX = 4
QW = REP * HD
QL = REP * BLK

SCALE = 168.0 ** (-0.5)
NEGATIVE = -1e30
MESH = pl.DeviceIdType.MESH
NT = (((1,), (1,)), ((), ()))
TN = (((0,), (0,)), ((), ()))
NN = (((1,), (0,)), ((), ()))


def mm(a, b, dims):
    return lax.dot_general(a, b, dims, preferred_element_type=jnp.float32)


def kernel(
    n_ctx, n_tp,
    q_ref, k_ref, v_ref, g_ref, len_ref, swap_ref,
    ao_ref, gq_ref, gk_ref, gv_ref,
    kb0, kb1, kb2, kb3, kb4, vb0, vb1, vb2, vb3, vb4, qb, gb, flags,
    ks, vs, qs, gs, sc, dp, pb, dsb,
    ob, dqb, part, own, mate, near, far, hub, relay,
    loc_sem, rk4_sem, rv4_sem, late_sem, send_sem, rk_sem, rv_sem, rq_sem, rf_sem, out_sem, pd_sem, hub_sem,
):
    kb = (kb0, kb1, kb2, kb3, kb4)
    vb = (vb0, vb1, vb2, vb3, vb4)
    p = lax.axis_index("dp")
    c = lax.axis_index("ctx")
    y = lax.axis_index("tp")
    other = 1 - p
    x = lax.rem(c, NX)
    ahead = lax.rem(c + NX, n_ctx)
    behind = lax.rem(c + n_ctx - NX, n_ctx)

    first = c < NX
    final = c + NX >= n_ctx

    def cols(ref, j, width):
        return ref.at[0, :, pl.ds(pl.multiple_of(j * width, width), width)]

    local = [
        pltpu.make_async_copy(cols(k_ref, p, HD), kb0.at[p], loc_sem.at[0]),
        pltpu.make_async_copy(cols(q_ref, p, QW), qb.at[p], loc_sem.at[1]),
        pltpu.make_async_copy(cols(v_ref, p, HD), vb0.at[p], loc_sem.at[2]),
        pltpu.make_async_copy(cols(g_ref, p, QW), gb.at[p], loc_sem.at[3]),
    ]
    for cp in local:
        cp.start()
    flags[0, 0] = swap_ref[0, 0]

    barrier = pltpu.get_barrier_semaphore()

    def greet(dev):
        pl.semaphore_signal(barrier, inc=1, device_id=dev, device_id_type=MESH)

    inner = jnp.logical_not(first)
    onward = jnp.logical_not(final)
    skip_on = (x >= NX // 2) & onward
    skip_back = (x < NX // 2) & inner
    side_on = (x == 1) & onward
    side_back = (x == 0) & inner

    latest = (p == 0) & (c == 0) & (y == 0)
    by_latest = jnp.logical_not(latest) & (((y == 0) & (c <= NX)) | (c == 0))

    @pl.when(jnp.logical_not(latest))
    def _():
        greet((other, c, y))
        for j in range(2):
            for d in range(1, NX):
                greet((j, c - x + lax.rem(x + d, NX), y))
            for d in range(1, n_tp):
                greet((j, c, lax.rem(y + d, n_tp)))
        for cond, dev in (
            (onward, ahead),
            (inner, behind),
            (skip_on, lax.rem(c + 2, n_ctx)),
            (skip_back, lax.rem(c + n_ctx - 2, n_ctx)),
            (side_on, lax.rem(c + 3, n_ctx)),
            (side_back, lax.rem(c + n_ctx - 3, n_ctx)),
        ):
            @pl.when(cond)
            def _():
                for j in range(2):
                    greet((j, dev, y))

    met = 1 + 2 * (NX - 1) + 2 * (n_tp - 1) - by_latest.astype(jnp.int32)
    for cond in (onward, inner, skip_on, skip_back, side_on, side_back):
        met = met + 2 * cond.astype(jnp.int32)
    pl.semaphore_wait(barrier, met)

    @pl.when(latest)
    def _():
        beside = [(1, 0, 0)]
        for j in range(2):
            beside += [(j, d, 0) for d in range(1, min(NX + 1, n_ctx))]
            beside += [(j, 0, t) for t in range(1, n_tp)]
        for dev in beside:
            pl.semaphore_signal(late_sem, inc=1, device_id=dev, device_id_type=MESH)

    def meet_latest(cond):
        @pl.when(by_latest & cond)
        def _():
            pl.semaphore_wait(late_sem, 1)

    count = [0]
    waits = []

    def remote(src, dst, recv, dev, cond=None):
        sem = send_sem.at[count[0]]
        count[0] += 1
        cp = pltpu.make_async_remote_copy(
            src_ref=src, dst_ref=dst, send_sem=sem, recv_sem=recv,
            device_id=dev, device_id_type=MESH,
        )
        if cond is None:
            cp.start()
        else:
            @pl.when(cond)
            def _():
                cp.start()
        waits.append((cp, cond))
        return cp

    def arrived(ref, sem, cond=None):
        if cond is None:
            pltpu.make_async_copy(ref, ref, sem).wait()
        else:
            @pl.when(cond)
            def _():
                pltpu.make_async_copy(ref, ref, sem).wait()

    mine = (other, c, y)

    def later(d):
        return lax.rem(c + d, n_ctx)

    def earlier(d):
        return lax.rem(c + n_ctx - d, n_ctx)

    def reaches(d):
        return c + 2 < n_ctx if d == 2 else onward if d == REACH else x + d < NX

    def starts(d):
        return (x == 0) | side_on if d == 3 else reaches(d)

    for d in (4, 1, 3, 2):
        remote(flags.at[0], flags.at[d], rf_sem.at[d], (p, later(d), y), starts(d))
    def send(pieces, cond=None):
        for src, dst, sem, d in pieces:
            for j in range(2):
                remote(
                    cols(src, j, HD), dst[d].at[p], sem.at[d], (j, later(d), y),
                    starts(d) if cond is None else cond,
                )

    def send_half(src, dst, sem, h):
        rows = pl.ds(h * (BLK // 2), BLK // 2)
        for j in range(2):
            remote(
                src.at[0, rows, pl.ds(j * HD, HD)], dst.at[p, rows], sem.at[h], (j, ahead, y), onward,
            )

    send_half(k_ref, kb4, rk4_sem, 0)
    send_half(k_ref, kb4, rk4_sem, 1)
    send([(k_ref, kb, rk_sem, 1), (k_ref, kb, rk_sem, 3)])
    send_half(v_ref, vb4, rv4_sem, 0)
    send_half(v_ref, vb4, rv4_sem, 1)
    send([(k_ref, kb, rk_sem, 2)], x < NX // 2)
    send([(v_ref, vb, rv_sem, 1), (v_ref, vb, rv_sem, 3)])
    send([(v_ref, vb, rv_sem, 2)], x < NX // 2)
    meet_latest((y == 0) & (c == 0))
    remote(cols(q_ref, other, QW), qb.at[p], rq_sem.at[0], mine)
    remote(cols(k_ref, other, HD), kb0.at[p], rk_sem.at[0], mine)
    remote(cols(g_ref, other, QW), gb.at[p], rq_sem.at[1], mine)
    remote(cols(v_ref, other, HD), vb0.at[p], rv_sem.at[0], mine)

    for d in range(1, REACH + 1):
        @pl.when(c < d)
        def _():
            flags[d, 0] = 0
            kb[d][...] = jnp.zeros_like(kb[d])
            vb[d][...] = jnp.zeros_like(vb[d])

    lane = lax.broadcasted_iota(jnp.int32, (1, BLK), 1)
    pos = c * BLK + lane
    lows = []
    for pi in range(2):
        low = jnp.maximum(pos - (W - 1), 0)
        end = jnp.int32(0)
        for r in range(len_ref.shape[1]):
            end = end + len_ref[pi, r]
            low = jnp.maximum(low, jnp.where(pos >= end, end, 0))
        lows.append(jnp.concatenate([low] * REP, axis=1) - c * BLK)
    lane2 = jnp.concatenate([lane] * REP, axis=1)
    row_id = lax.broadcasted_iota(jnp.int32, (BLK, QL), 0)

    def pick(ref, swapped, pi):
        a, b = ref[pi], ref[1 - pi]
        return jnp.where(swapped, b, a)

    def take(d):
        swapped = (swap_ref[0, 0] if d == 0 else flags[d, 0]) == 1
        for pi in range(2):
            key = pick(kb[d], swapped, pi)
            ks[pi, d] = key
            s = mm(key, qs[pi], NT) * SCALE
            ok = row_id - d * BLK >= lows[pi]
            if d == 0:
                ok = ok & (row_id <= lane2)
            sc[pi, d] = jnp.where(ok, s, NEGATIVE)

    def take_v(d):
        swapped = (swap_ref[0, 0] if d == 0 else flags[d, 0]) == 1
        for pi in range(2):
            val = pick(vb[d], swapped, pi)
            vs[pi, d] = val
            dp[pi, d] = mm(val, gs[pi], NT)

    def stack(src, dst, swapped):
        for pi in range(2):
            t = pick(src, swapped, pi)
            for r in range(REP):
                dst[pi, r * BLK:(r + 1) * BLK] = t[:, r * HD:(r + 1) * HD]

    for cp in local:
        cp.wait()
    swapped = swap_ref[0, 0] == 1
    arrived(qb.at[other], rq_sem.at[0])
    stack(qb, qs, swapped)
    arrived(kb0.at[other], rk_sem.at[0])
    take(0)
    arrived(gb.at[other], rq_sem.at[1])
    stack(gb, gs, swapped)

    relays = inner & (x >= 2)

    def pass_halves(buf, sem, own_sem):
        for h in range(2):
            rows = pl.ds(h * (BLK // 2), BLK // 2)
            arrived(buf[4].at[:, rows], own_sem.at[h], relays)
            for e in (3, 1):
                remote(
                    buf[4].at[:, rows], buf[4 - e].at[:, rows], sem.at[4 - e],
                    (p, earlier(e), y), inner & (x >= max(e, 2)),
                )
            if h == 0 and own_sem is rk4_sem:
                send([(k_ref, kb, rk_sem, 2), (v_ref, vb, rv_sem, 2)], skip_on)

    def last_halves(buf, own_sem):
        for h in range(2):
            rows = pl.ds(h * (BLK // 2), BLK // 2)
            arrived(buf[4].at[:, rows], own_sem.at[h], inner & (x < 2))

    arrived(flags.at[4], rf_sem.at[4], relays)
    for e in (1, 3):
        remote(flags.at[4], flags.at[4 - e], rf_sem.at[4 - e], (p, earlier(e), y), inner & (x >= max(e, 2)))
    pass_halves(kb, rk_sem, rk4_sem)
    pass_halves(vb, rv_sem, rv4_sem)
    arrived(vb0.at[other], rv_sem.at[0])
    take_v(0)
    for d in (2, 3, 1):
        arrived(flags.at[d], rf_sem.at[d], c >= d)
        arrived(kb[d], rk_sem.at[d], c >= d)
        take(d)
    arrived(flags.at[4], rf_sem.at[4], inner & (x < 2))
    last_halves(kb, rk4_sem)
    take(4)

    def give(s, d, pi):
        direct = c >= 2 if d == 2 else x >= d
        remote(part.at[d, s, pi], near.at[d - 1, s, p], pd_sem.at[s, d], (pi, earlier(d), y), direct)
        if d != 2:
            remote(
                part.at[d, s, pi], relay.at[NX - d - 1, s, pi], hub_sem.at[s, pi, NX - d],
                (p, c + NX - d, y), inner & (x < d),
            )

    def hand_back(s, pi, cond):
        @pl.when(cond)
        def _():
            part[4, s, pi] = hub[s, pi].astype(jnp.bfloat16)
        remote(part.at[4, s, pi], far.at[s, p], pd_sem.at[s, 4], (pi, behind, y), inner & cond)

    meet_latest((y == 0) & (c > 0))
    for pi in range(2):
        top = jnp.max(sc[pi, 0], axis=0, keepdims=True)
        for d in range(1, REACH + 1):
            top = jnp.maximum(top, jnp.max(sc[pi, d], axis=0, keepdims=True))
        total = jnp.zeros((1, QL), jnp.float32)
        for d in range(REACH + 1):
            e = jnp.exp(sc[pi, d] - top)
            sc[pi, d] = e
            total = total + jnp.sum(e, axis=0, keepdims=True)
        inv = 1.0 / total
        for d in (1, 3, 2, 4, 0):
            pr = sc[pi, d] * inv
            sc[pi, d] = pr
            pb[pi, d] = pr.astype(jnp.bfloat16)
            dv = mm(pb[pi, d], gs[pi], NN)
            if d == 0:
                own[1, pi] = dv
            elif d == 4:
                hub[1, pi] = dv
            else:
                part[d, 1, pi] = dv.astype(jnp.bfloat16)
        for d in (1, 3):
            give(1, d, pi)
        hand_back(1, pi, x < 1)
    for pi in range(2):
        give(1, 2, pi)
    remote(own.at[1, other], mate.at[1], pd_sem.at[1, 0], mine)

    for d in (2, 3, 1):
        arrived(vb[d], rv_sem.at[d], c >= d)
        take_v(d)
    last_halves(vb, rv4_sem)
    take_v(4)
    for pi in range(2):
        delta = jnp.zeros((1, QL), jnp.float32)
        for d in range(REACH + 1):
            delta = delta + jnp.sum(sc[pi, d] * dp[pi, d], axis=0, keepdims=True)
        for d in (1, 3, 2, 4, 0):
            dsb[pi, d] = (sc[pi, d] * (dp[pi, d] - delta)).astype(jnp.bfloat16)
            dk = mm(dsb[pi, d], qs[pi], NN) * SCALE
            if d == 0:
                own[0, pi] = dk
            elif d == 4:
                hub[0, pi] = dk
            else:
                part[d, 0, pi] = dk.astype(jnp.bfloat16)
        for d in (1, 3):
            give(0, d, pi)
        hand_back(0, pi, x < 1)
    remote(own.at[0, other], mate.at[0], pd_sem.at[0, 0], mine)

    for pi in range(2):
        o = (mm(dsb[pi].reshape(-1, QL), ks[pi].reshape(-1, HD), TN) * SCALE).astype(jnp.bfloat16)
        for r in range(REP):
            dqb[pi, :, r * HD:(r + 1) * HD] = o[r * BLK:(r + 1) * BLK]
    keep_q = pltpu.make_async_copy(dqb.at[p], cols(gq_ref, p, QW), loc_sem.at[6])
    keep_q.start()
    remote(dqb.at[other], cols(gq_ref, p, QW), out_sem.at[1], mine)
    for pi in range(2):
        o = mm(pb[pi].reshape(-1, QL), vs[pi].reshape(-1, HD), TN).astype(jnp.bfloat16)
        for r in range(REP):
            ob[pi, :, r * HD:(r + 1) * HD] = o[r * BLK:(r + 1) * BLK]
    meet_latest(y > 0)
    share = BLK // n_tp
    width = REP * HD
    at = pl.ds(pl.multiple_of((y * 2 + p) * width, width), width)
    for dt in range(n_tp):
        t = lax.rem(y + dt, n_tp)
        rows = pl.ds(pl.multiple_of(t * share, share), share)
        for dj in range(2):
            pi = p if dj == 0 else other
            if dt == 0 and dj == 0:
                keep = pltpu.make_async_copy(ob.at[pi, rows], ao_ref.at[0, :, at], loc_sem.at[5])
                keep.start()
            else:
                remote(ob.at[pi, rows], ao_ref.at[0, :, at], out_sem.at[0], (pi, c, t))

    for pi in range(2):
        give(0, 2, pi)

    for s in (1, 0):
        for pi in range(2):
            for e in (1, 3):
                @pl.when(inner & (x >= e))
                def _():
                    arrived(relay.at[e - 1, s, pi], hub_sem.at[s, pi, e])
                    hub[s, pi] = hub[s, pi] + relay[e - 1, s, pi].astype(jnp.float32)
            hand_back(s, pi, x >= 1)

    for s, out in ((1, gv_ref), (0, gk_ref)):
        arrived(mate.at[s], pd_sem.at[s, 0])
        for d in range(1, NX):
            @pl.when(reaches(d))
            def _():
                arrived(near.at[d - 1, s], pd_sem.at[s, d])
                own[s, p] = own[s, p] + near[d - 1, s, p].astype(jnp.float32)
                mate[s] = mate[s] + near[d - 1, s, other].astype(jnp.float32)

        @pl.when(onward)
        def _():
            arrived(far.at[s], pd_sem.at[s, 4])
            own[s, p] = own[s, p] + far[s, p].astype(jnp.float32)
            mate[s] = mate[s] + far[s, other].astype(jnp.float32)
        for j, src in ((p, own[s, p]), (other, mate[s])):
            out[0, :, pl.ds(pl.multiple_of(j * HD, HD), HD)] = src.astype(jnp.bfloat16)

    keep.wait()
    keep_q.wait()
    arrived(ao_ref.at[0, :, pl.ds(0, (2 * n_tp - 1) * width)], out_sem.at[0])
    arrived(cols(gq_ref, other, QW), out_sem.at[1])
    for cp, cond in waits:
        if cond is None:
            cp.wait_send()
        else:
            @pl.when(cond)
            def _():
                cp.wait_send()


def store(a_ref, b_ref, c_ref, d_ref, ao_ref, gq_ref, gk_ref, gv_ref, sem):
    copies = [
        pltpu.make_async_copy(src, dst, sem.at[i])
        for i, (src, dst) in enumerate(((a_ref, ao_ref), (b_ref, gq_ref), (c_ref, gk_ref), (d_ref, gv_ref)))
    ]
    for cp in copies:
        cp.start()
    for cp in copies:
        cp.wait()


def body(n_ctx, n_tp, queries, key_rows, values, grad_out, lengths, pair_swap):
    bf, f32 = jnp.bfloat16, jnp.float32
    nd = REACH + 1
    kv_piece = pltpu.VMEM((2, BLK, HD), bf)
    any_spec = pl.BlockSpec(memory_space=pl.ANY)
    vmem_spec = pl.BlockSpec(memory_space=pltpu.VMEM)
    dma = pltpu.SemaphoreType.DMA
    shapes = (
        ((1, BLK // n_tp, n_tp * 2 * QW), bf),
        (queries.shape, bf),
        (key_rows.shape, bf),
        (values.shape, bf),
    )
    held = pl.pallas_call(
        functools.partial(kernel, n_ctx, n_tp),
        out_shape=tuple(pltpu.VMEM(*item) for item in shapes),
        in_specs=[any_spec] * 4 + [pl.BlockSpec(memory_space=pltpu.SMEM)] * 2,
        out_specs=(vmem_spec,) * 4,
        scratch_shapes=[kv_piece] * 10 + [
            pltpu.VMEM((2, BLK, QW), bf),
            pltpu.VMEM((2, BLK, QW), bf),
            pltpu.SMEM((nd, 1), jnp.int32),
            pltpu.VMEM((2, nd, BLK, HD), bf),
            pltpu.VMEM((2, nd, BLK, HD), bf),
            pltpu.VMEM((2, QL, HD), bf),
            pltpu.VMEM((2, QL, HD), bf),
            pltpu.VMEM((2, nd, BLK, QL), f32),
            pltpu.VMEM((2, nd, BLK, QL), f32),
            pltpu.VMEM((2, nd, BLK, QL), bf),
            pltpu.VMEM((2, nd, BLK, QL), bf),
            pltpu.VMEM((2, BLK, QW), bf),
            pltpu.VMEM((2, BLK, QW), bf),
            pltpu.VMEM((nd, 2, 2, BLK, HD), bf),
            pltpu.VMEM((2, 2, BLK, HD), f32),
            pltpu.VMEM((2, BLK, HD), f32),
            pltpu.VMEM((3, 2, 2, BLK, HD), bf),
            pltpu.VMEM((2, 2, BLK, HD), bf),
            pltpu.VMEM((2, 2, BLK, HD), f32),
            pltpu.VMEM((3, 2, 2, BLK, HD), bf),
            dma((7,)),
            dma((2,)),
            dma((2,)),
            pltpu.SemaphoreType.REGULAR,
            dma((100,)),
            dma((nd,)),
            dma((nd,)),
            dma((2,)),
            dma((nd,)),
            dma((2,)),
            dma((2, nd)),
            dma((2, 2, NX)),
        ],
        compiler_params=pltpu.CompilerParams(collective_id=0, has_side_effects=True),
        name="attend",
    )(queries, key_rows, values, grad_out, lengths, pair_swap.reshape(1, 1))
    return pl.pallas_call(
        store,
        out_shape=tuple(jax.ShapeDtypeStruct(*item) for item in shapes),
        in_specs=[any_spec] * 4,
        out_specs=(any_spec,) * 4,
        scratch_shapes=[dma((4,))],
        name="store",
    )(*[pltpu.with_memory_space_constraint(item, pltpu.VMEM) for item in held])


def solution(mesh):
    placed = P("dp", "ctx", "tp")
    return jax.shard_map(
        functools.partial(body, mesh.shape["ctx"], mesh.shape["tp"]),
        mesh=mesh,
        in_specs=(placed, placed, placed, placed, P(), P("ctx")),
        out_specs=(P("dp", ("ctx", "tp"), None), placed, placed, placed),
        check_vma=False,
    )
```

```python
import functools

import jax
import jax.numpy as jnp
from jax import lax
from jax.experimental import pallas as pl
from jax.experimental.pallas import tpu as pltpu
from jax.sharding import PartitionSpec as P

HD = 128
REP = 2
W = 512
BLK = 128
REACH = W // BLK
NX = 4
QW = REP * HD
QL = REP * BLK

SCALE = 168.0 ** (-0.5)
NEGATIVE = -1e30
MESH = pl.DeviceIdType.MESH
NT = (((1,), (1,)), ((), ()))
TN = (((0,), (0,)), ((), ()))
NN = (((1,), (0,)), ((), ()))


def mm(a, b, dims):
    return lax.dot_general(a, b, dims, preferred_element_type=jnp.float32)


def kernel(
    n_ctx, n_tp,
    q_ref, k_ref, v_ref, g_ref, len_ref, swap_ref,
    ao_ref, gq_ref, gk_ref, gv_ref,
    kb0, kb1, kb2, kb3, kb4, vb0, vb1, vb2, vb3, vb4, qb, gb, flags,
    ks, vs, qs, gs, sc, dp, pb, dsb,
    ob, dqb, part, own, mate, near, far, hub, relay,
    loc_sem, rk4_sem, rv4_sem, late_sem, send_sem, rk_sem, rv_sem, rq_sem, rf_sem, out_sem, pd_sem, hub_sem,
):
    kb = (kb0, kb1, kb2, kb3, kb4)
    vb = (vb0, vb1, vb2, vb3, vb4)
    p = lax.axis_index("dp")
    c = lax.axis_index("ctx")
    y = lax.axis_index("tp")
    other = 1 - p
    x = lax.rem(c, NX)
    ahead = lax.rem(c + NX, n_ctx)
    behind = lax.rem(c + n_ctx - NX, n_ctx)

    first = c < NX
    final = c + NX >= n_ctx

    def cols(ref, j, width):
        return ref.at[0, :, pl.ds(pl.multiple_of(j * width, width), width)]

    local = [
        pltpu.make_async_copy(cols(k_ref, p, HD), kb0.at[p], loc_sem.at[0]),
        pltpu.make_async_copy(cols(q_ref, p, QW), qb.at[p], loc_sem.at[1]),
        pltpu.make_async_copy(cols(v_ref, p, HD), vb0.at[p], loc_sem.at[2]),
        pltpu.make_async_copy(cols(g_ref, p, QW), gb.at[p], loc_sem.at[3]),
    ]
    for cp in local:
        cp.start()
    flags[0, 0] = swap_ref[0, 0]

    barrier = pltpu.get_barrier_semaphore()

    def greet(dev):
        pl.semaphore_signal(barrier, inc=1, device_id=dev, device_id_type=MESH)

    inner = jnp.logical_not(first)
    onward = jnp.logical_not(final)
    skip_on = (x >= NX // 2) & onward
    skip_back = (x < NX // 2) & inner
    side_on = (x == 1) & onward
    side_back = (x == 0) & inner
    wrap_on = (x == NX - 1) & onward
    third_back = (x == 2) & inner

    latest = (p == 0) & (c == 0) & (y == 0)
    by_latest = jnp.logical_not(latest) & (((y == 0) & (c <= NX)) | (c == 0))

    @pl.when(jnp.logical_not(latest))
    def _():
        greet((other, c, y))
        for j in range(2):
            for d in range(1, NX):
                greet((j, c - x + lax.rem(x + d, NX), y))
            for d in range(1, n_tp):
                greet((j, c, lax.rem(y + d, n_tp)))
        for cond, dev in (
            (onward, ahead),
            (inner, behind),
            (skip_on, lax.rem(c + 2, n_ctx)),
            (skip_back, lax.rem(c + n_ctx - 2, n_ctx)),
            (side_on, lax.rem(c + 3, n_ctx)),
            (side_back, lax.rem(c + n_ctx - 3, n_ctx)),
            (wrap_on, lax.rem(c + 1, n_ctx)),
            (wrap_on, lax.rem(c + 3, n_ctx)),
            (third_back, lax.rem(c + n_ctx - 3, n_ctx)),
            (side_back, lax.rem(c + n_ctx - 1, n_ctx)),
        ):
            @pl.when(cond)
            def _():
                for j in range(2):
                    greet((j, dev, y))

    met = 1 + 2 * (NX - 1) + 2 * (n_tp - 1) - by_latest.astype(jnp.int32)
    for cond in (onward, inner, skip_on, skip_back, side_on, side_back, wrap_on, side_back, wrap_on, third_back):
        met = met + 2 * cond.astype(jnp.int32)
    pl.semaphore_wait(barrier, met)

    @pl.when(latest)
    def _():
        beside = [(1, 0, 0)]
        for j in range(2):
            beside += [(j, d, 0) for d in range(1, min(NX + 1, n_ctx))]
            beside += [(j, 0, t) for t in range(1, n_tp)]
        for dev in beside:
            pl.semaphore_signal(late_sem, inc=1, device_id=dev, device_id_type=MESH)

    def meet_latest(cond):
        @pl.when(by_latest & cond)
        def _():
            pl.semaphore_wait(late_sem, 1)

    count = [0]
    waits = []

    def remote(src, dst, recv, dev, cond=None):
        sem = send_sem.at[count[0]]
        count[0] += 1
        cp = pltpu.make_async_remote_copy(
            src_ref=src, dst_ref=dst, send_sem=sem, recv_sem=recv,
            device_id=dev, device_id_type=MESH,
        )
        if cond is None:
            cp.start()
        else:
            @pl.when(cond)
            def _():
                cp.start()
        waits.append((cp, cond))
        return cp

    def arrived(ref, sem, cond=None):
        if cond is None:
            pltpu.make_async_copy(ref, ref, sem).wait()
        else:
            @pl.when(cond)
            def _():
                pltpu.make_async_copy(ref, ref, sem).wait()

    mine = (other, c, y)

    def later(d):
        return lax.rem(c + d, n_ctx)

    def earlier(d):
        return lax.rem(c + n_ctx - d, n_ctx)

    def reaches(d):
        return c + 2 < n_ctx if d == 2 else onward if d == REACH else x + d < NX

    def starts(d):
        return (x == 0) | side_on if d == 3 else reaches(d)

    for d in (4, 1, 3, 2):
        remote(flags.at[0], flags.at[d], rf_sem.at[d], (p, later(d), y), starts(d))
    def send(pieces, cond=None):
        for src, dst, sem, d in pieces:
            for j in range(2):
                remote(
                    cols(src, j, HD), dst[d].at[p], sem.at[d], (j, later(d), y),
                    starts(d) if cond is None else cond,
                )

    def send_half(src, dst, sem, h):
        rows = pl.ds(h * (BLK // 2), BLK // 2)
        for j in range(2):
            remote(
                src.at[0, rows, pl.ds(j * HD, HD)], dst.at[p, rows], sem.at[h], (j, ahead, y), onward,
            )

    send_half(k_ref, kb4, rk4_sem, 0)
    send_half(k_ref, kb4, rk4_sem, 1)
    send([(k_ref, kb, rk_sem, 1), (k_ref, kb, rk_sem, 3)])
    send_half(v_ref, vb4, rv4_sem, 0)
    send_half(v_ref, vb4, rv4_sem, 1)
    send([(k_ref, kb, rk_sem, 2)], x < NX // 2)
    send([(v_ref, vb, rv_sem, 1), (v_ref, vb, rv_sem, 3)])
    send([(v_ref, vb, rv_sem, 2)], x < NX // 2)
    meet_latest((y == 0) & (c == 0))
    remote(cols(q_ref, other, QW), qb.at[p], rq_sem.at[0], mine)
    remote(cols(k_ref, other, HD), kb0.at[p], rk_sem.at[0], mine)
    remote(cols(g_ref, other, QW), gb.at[p], rq_sem.at[1], mine)
    remote(cols(v_ref, other, HD), vb0.at[p], rv_sem.at[0], mine)

    for d in range(1, REACH + 1):
        @pl.when(c < d)
        def _():
            flags[d, 0] = 0
            kb[d][...] = jnp.zeros_like(kb[d])
            vb[d][...] = jnp.zeros_like(vb[d])

    lane = lax.broadcasted_iota(jnp.int32, (1, BLK), 1)
    pos = c * BLK + lane
    lows = []
    for pi in range(2):
        low = jnp.maximum(pos - (W - 1), 0)
        end = jnp.int32(0)
        for r in range(len_ref.shape[1]):
            end = end + len_ref[pi, r]
            low = jnp.maximum(low, jnp.where(pos >= end, end, 0))
        lows.append(jnp.concatenate([low] * REP, axis=1) - c * BLK)
    lane2 = jnp.concatenate([lane] * REP, axis=1)
    row_id = lax.broadcasted_iota(jnp.int32, (BLK, QL), 0)

    def pick(ref, swapped, pi):
        a, b = ref[pi], ref[1 - pi]
        return jnp.where(swapped, b, a)

    def take(d):
        swapped = (swap_ref[0, 0] if d == 0 else flags[d, 0]) == 1
        for pi in range(2):
            key = pick(kb[d], swapped, pi)
            ks[pi, d] = key
            s = mm(key, qs[pi], NT) * SCALE
            ok = row_id - d * BLK >= lows[pi]
            if d == 0:
                ok = ok & (row_id <= lane2)
            sc[pi, d] = jnp.where(ok, s, NEGATIVE)

    def take_v(d):
        swapped = (swap_ref[0, 0] if d == 0 else flags[d, 0]) == 1
        for pi in range(2):
            val = pick(vb[d], swapped, pi)
            vs[pi, d] = val
            dp[pi, d] = mm(val, gs[pi], NT)

    def stack(src, dst, swapped):
        for pi in range(2):
            t = pick(src, swapped, pi)
            for r in range(REP):
                dst[pi, r * BLK:(r + 1) * BLK] = t[:, r * HD:(r + 1) * HD]

    for cp in local:
        cp.wait()
    swapped = swap_ref[0, 0] == 1
    arrived(qb.at[other], rq_sem.at[0])
    stack(qb, qs, swapped)
    arrived(kb0.at[other], rk_sem.at[0])
    take(0)
    arrived(gb.at[other], rq_sem.at[1])
    stack(gb, gs, swapped)

    relays = inner & (x >= 2)

    def pass_halves(buf, sem, own_sem):
        for h in range(2):
            rows = pl.ds(h * (BLK // 2), BLK // 2)
            arrived(buf[4].at[:, rows], own_sem.at[h], relays)
            for e in (3, 1):
                remote(
                    buf[4].at[:, rows], buf[4 - e].at[:, rows], sem.at[4 - e],
                    (p, earlier(e), y), inner & (x >= max(e, 2)),
                )
            if h == 0 and own_sem is rk4_sem:
                send([(k_ref, kb, rk_sem, 2), (v_ref, vb, rv_sem, 2)], skip_on)

    def last_halves(buf, own_sem):
        for h in range(2):
            rows = pl.ds(h * (BLK // 2), BLK // 2)
            arrived(buf[4].at[:, rows], own_sem.at[h], inner & (x < 2))

    arrived(flags.at[4], rf_sem.at[4], relays)
    for e in (1, 3):
        remote(flags.at[4], flags.at[4 - e], rf_sem.at[4 - e], (p, earlier(e), y), inner & (x >= max(e, 2)))
    pass_halves(kb, rk_sem, rk4_sem)
    pass_halves(vb, rv_sem, rv4_sem)
    arrived(vb0.at[other], rv_sem.at[0])
    take_v(0)
    for d in (2, 3, 1):
        arrived(flags.at[d], rf_sem.at[d], c >= d)
        arrived(kb[d], rk_sem.at[d], c >= d)
        take(d)
    arrived(flags.at[4], rf_sem.at[4], inner & (x < 2))
    last_halves(kb, rk4_sem)
    take(4)

    def give(s, d, pi):
        straight = d == 1 and s == 0
        direct = c >= d if d == 2 or straight else x >= d
        if d == 3 and s == 0:
            direct = direct | third_back
        remote(part.at[d, s, pi], near.at[d - 1, s, p], pd_sem.at[s, d], (pi, earlier(d), y), direct)
        if d == 3 or (d == 1 and not straight):
            remote(
                part.at[d, s, pi], relay.at[NX - d - 1, s, pi], hub_sem.at[s, pi, NX - d],
                (p, c + NX - d, y), inner & (x < (2 if s == 0 else d)),
            )

    def hand_back(s, pi, cond):
        @pl.when(cond)
        def _():
            part[4, s, pi] = hub[s, pi].astype(jnp.bfloat16)
        remote(part.at[4, s, pi], far.at[s, p], pd_sem.at[s, 4], (pi, behind, y), inner & cond)

    meet_latest((y == 0) & (c > 0))
    for pi in range(2):
        top = jnp.max(sc[pi, 0], axis=0, keepdims=True)
        for d in range(1, REACH + 1):
            top = jnp.maximum(top, jnp.max(sc[pi, d], axis=0, keepdims=True))
        total = jnp.zeros((1, QL), jnp.float32)
        for d in range(REACH + 1):
            e = jnp.exp(sc[pi, d] - top)
            sc[pi, d] = e
            total = total + jnp.sum(e, axis=0, keepdims=True)
        inv = 1.0 / total
        for d in (1, 3, 2, 4, 0):
            pr = sc[pi, d] * inv
            sc[pi, d] = pr
            pb[pi, d] = pr.astype(jnp.bfloat16)
            dv = mm(pb[pi, d], gs[pi], NN)
            if d == 0:
                own[1, pi] = dv
            elif d == 4:
                hub[1, pi] = dv
            else:
                part[d, 1, pi] = dv.astype(jnp.bfloat16)
        for d in (1, 3):
            give(1, d, pi)
        hand_back(1, pi, x < 1)
    for pi in range(2):
        give(1, 2, pi)
    remote(own.at[1, other], mate.at[1], pd_sem.at[1, 0], mine)

    for d in (2, 3, 1):
        arrived(vb[d], rv_sem.at[d], c >= d)
        take_v(d)
    last_halves(vb, rv4_sem)
    take_v(4)
    for pi in range(2):
        delta = jnp.zeros((1, QL), jnp.float32)
        for d in range(REACH + 1):
            delta = delta + jnp.sum(sc[pi, d] * dp[pi, d], axis=0, keepdims=True)
        for d in (1, 3, 2, 4, 0):
            dsb[pi, d] = (sc[pi, d] * (dp[pi, d] - delta)).astype(jnp.bfloat16)
            dk = mm(dsb[pi, d], qs[pi], NN) * SCALE
            if d == 0:
                own[0, pi] = dk
            elif d == 4:
                hub[0, pi] = dk
            else:
                part[d, 0, pi] = dk.astype(jnp.bfloat16)
        for d in (1, 3):
            give(0, d, pi)
        hand_back(0, pi, (x == 0) | (x == NX - 1))
    remote(own.at[0, other], mate.at[0], pd_sem.at[0, 0], mine)

    for pi in range(2):
        o = (mm(dsb[pi].reshape(-1, QL), ks[pi].reshape(-1, HD), TN) * SCALE).astype(jnp.bfloat16)
        for r in range(REP):
            dqb[pi, :, r * HD:(r + 1) * HD] = o[r * BLK:(r + 1) * BLK]
    keep_q = pltpu.make_async_copy(dqb.at[p], cols(gq_ref, p, QW), loc_sem.at[6])
    keep_q.start()
    remote(dqb.at[other], cols(gq_ref, p, QW), out_sem.at[1], mine)
    for pi in range(2):
        o = mm(pb[pi].reshape(-1, QL), vs[pi].reshape(-1, HD), TN).astype(jnp.bfloat16)
        for r in range(REP):
            ob[pi, :, r * HD:(r + 1) * HD] = o[r * BLK:(r + 1) * BLK]
    meet_latest(y > 0)
    share = BLK // n_tp
    width = REP * HD
    at = pl.ds(pl.multiple_of((y * 2 + p) * width, width), width)
    for dt in range(n_tp):
        t = lax.rem(y + dt, n_tp)
        rows = pl.ds(pl.multiple_of(t * share, share), share)
        for dj in range(2):
            pi = p if dj == 0 else other
            if dt == 0 and dj == 0:
                keep = pltpu.make_async_copy(ob.at[pi, rows], ao_ref.at[0, :, at], loc_sem.at[5])
                keep.start()
            else:
                remote(ob.at[pi, rows], ao_ref.at[0, :, at], out_sem.at[0], (pi, c, t))

    for pi in range(2):
        give(0, 2, pi)

    for s in (1, 0):
        for pi in range(2):
            for e in (1, 3):
                if s == 0 and e == 3:
                    continue

                @pl.when(inner & (x >= e) & (x < (NX - 1 if s == 0 else NX)))
                def _():
                    arrived(relay.at[e - 1, s, pi], hub_sem.at[s, pi, e])
                    hub[s, pi] = hub[s, pi] + relay[e - 1, s, pi].astype(jnp.float32)
            hand_back(s, pi, (x >= 1) & (x < (NX - 1 if s == 0 else NX)))

    for s, out in ((1, gv_ref), (0, gk_ref)):
        arrived(mate.at[s], pd_sem.at[s, 0])
        for d in range(1, NX):
            @pl.when(reaches(d) | (wrap_on if d != 2 and s == 0 else reaches(d)))
            def _():
                arrived(near.at[d - 1, s], pd_sem.at[s, d])
                own[s, p] = own[s, p] + near[d - 1, s, p].astype(jnp.float32)
                mate[s] = mate[s] + near[d - 1, s, other].astype(jnp.float32)

        @pl.when(onward)
        def _():
            arrived(far.at[s], pd_sem.at[s, 4])
            own[s, p] = own[s, p] + far[s, p].astype(jnp.float32)
            mate[s] = mate[s] + far[s, other].astype(jnp.float32)
        for j, src in ((p, own[s, p]), (other, mate[s])):
            out[0, :, pl.ds(pl.multiple_of(j * HD, HD), HD)] = src.astype(jnp.bfloat16)

    keep.wait()
    keep_q.wait()
    arrived(ao_ref.at[0, :, pl.ds(0, (2 * n_tp - 1) * width)], out_sem.at[0])
    arrived(cols(gq_ref, other, QW), out_sem.at[1])
    for cp, cond in waits:
        if cond is None:
            cp.wait_send()
        else:
            @pl.when(cond)
            def _():
                cp.wait_send()


def store(a_ref, b_ref, c_ref, d_ref, ao_ref, gq_ref, gk_ref, gv_ref, sem):
    copies = [
        pltpu.make_async_copy(src, dst, sem.at[i])
        for i, (src, dst) in enumerate(((a_ref, ao_ref), (b_ref, gq_ref), (c_ref, gk_ref), (d_ref, gv_ref)))
    ]
    for cp in copies:
        cp.start()
    for cp in copies:
        cp.wait()


def body(n_ctx, n_tp, queries, key_rows, values, grad_out, lengths, pair_swap):
    bf, f32 = jnp.bfloat16, jnp.float32
    nd = REACH + 1
    kv_piece = pltpu.VMEM((2, BLK, HD), bf)
    any_spec = pl.BlockSpec(memory_space=pl.ANY)
    vmem_spec = pl.BlockSpec(memory_space=pltpu.VMEM)
    dma = pltpu.SemaphoreType.DMA
    shapes = (
        ((1, BLK // n_tp, n_tp * 2 * QW), bf),
        (queries.shape, bf),
        (key_rows.shape, bf),
        (values.shape, bf),
    )
    held = pl.pallas_call(
        functools.partial(kernel, n_ctx, n_tp),
        out_shape=tuple(pltpu.VMEM(*item) for item in shapes),
        in_specs=[any_spec] * 4 + [pl.BlockSpec(memory_space=pltpu.SMEM)] * 2,
        out_specs=(vmem_spec,) * 4,
        scratch_shapes=[kv_piece] * 10 + [
            pltpu.VMEM((2, BLK, QW), bf),
            pltpu.VMEM((2, BLK, QW), bf),
            pltpu.SMEM((nd, 1), jnp.int32),
            pltpu.VMEM((2, nd, BLK, HD), bf),
            pltpu.VMEM((2, nd, BLK, HD), bf),
            pltpu.VMEM((2, QL, HD), bf),
            pltpu.VMEM((2, QL, HD), bf),
            pltpu.VMEM((2, nd, BLK, QL), f32),
            pltpu.VMEM((2, nd, BLK, QL), f32),
            pltpu.VMEM((2, nd, BLK, QL), bf),
            pltpu.VMEM((2, nd, BLK, QL), bf),
            pltpu.VMEM((2, BLK, QW), bf),
            pltpu.VMEM((2, BLK, QW), bf),
            pltpu.VMEM((nd, 2, 2, BLK, HD), bf),
            pltpu.VMEM((2, 2, BLK, HD), f32),
            pltpu.VMEM((2, BLK, HD), f32),
            pltpu.VMEM((3, 2, 2, BLK, HD), bf),
            pltpu.VMEM((2, 2, BLK, HD), bf),
            pltpu.VMEM((2, 2, BLK, HD), f32),
            pltpu.VMEM((3, 2, 2, BLK, HD), bf),
            dma((7,)),
            dma((2,)),
            dma((2,)),
            pltpu.SemaphoreType.REGULAR,
            dma((100,)),
            dma((nd,)),
            dma((nd,)),
            dma((2,)),
            dma((nd,)),
            dma((2,)),
            dma((2, nd)),
            dma((2, 2, NX)),
        ],
        compiler_params=pltpu.CompilerParams(collective_id=0, has_side_effects=True),
        name="attend",
    )(queries, key_rows, values, grad_out, lengths, pair_swap.reshape(1, 1))
    return pl.pallas_call(
        store,
        out_shape=tuple(jax.ShapeDtypeStruct(*item) for item in shapes),
        in_specs=[any_spec] * 4,
        out_specs=(any_spec,) * 4,
        scratch_shapes=[dma((4,))],
        name="store",
    )(*[pltpu.with_memory_space_constraint(item, pltpu.VMEM) for item in held])


def solution(mesh):
    placed = P("dp", "ctx", "tp")
    return jax.shard_map(
        functools.partial(body, mesh.shape["ctx"], mesh.shape["tp"]),
        mesh=mesh,
        in_specs=(placed, placed, placed, placed, P(), P("ctx")),
        out_specs=(P("dp", ("ctx", "tp"), None), placed, placed, placed),
        check_vma=False,
    )
```

```python
import functools

import jax
import jax.numpy as jnp
from jax import lax
from jax.experimental import pallas as pl
from jax.experimental.pallas import tpu as pltpu
from jax.sharding import PartitionSpec as P

HD = 128
REP = 2
W = 512
BLK = 128
REACH = W // BLK
NX = 4
QW = REP * HD
QL = REP * BLK

SCALE = 168.0 ** (-0.5)
NEGATIVE = -1e30
MESH = pl.DeviceIdType.MESH
NT = (((1,), (1,)), ((), ()))
TN = (((0,), (0,)), ((), ()))
NN = (((1,), (0,)), ((), ()))


def mm(a, b, dims):
    return lax.dot_general(a, b, dims, preferred_element_type=jnp.float32)


def kernel(
    n_ctx, n_tp,
    q_ref, k_ref, v_ref, g_ref, len_ref, swap_ref,
    ao_ref, gq_ref, gk_ref, gv_ref,
    kb0, kb1, kb2, kb3, kb4, vb0, vb1, vb2, vb3, vb4, qb, gb, flags,
    ks, vs, qs, gs, sc, dp, pb, dsb,
    ob, dqb, part, own, mate, near, far, hub, relay,
    loc_sem, rk4_sem, rv4_sem, late_sem, send_sem, rk_sem, rv_sem, rq_sem, rf_sem, out_sem, pd_sem, hub_sem,
):
    kb = (kb0, kb1, kb2, kb3, kb4)
    vb = (vb0, vb1, vb2, vb3, vb4)
    p = lax.axis_index("dp")
    c = lax.axis_index("ctx")
    y = lax.axis_index("tp")
    other = 1 - p
    x = lax.rem(c, NX)
    ahead = lax.rem(c + NX, n_ctx)
    behind = lax.rem(c + n_ctx - NX, n_ctx)

    first = c < NX
    final = c + NX >= n_ctx

    def cols(ref, j, width):
        return ref.at[0, :, pl.ds(pl.multiple_of(j * width, width), width)]

    local = [
        pltpu.make_async_copy(cols(k_ref, p, HD), kb0.at[p], loc_sem.at[0]),
        pltpu.make_async_copy(cols(q_ref, p, QW), qb.at[p], loc_sem.at[1]),
        pltpu.make_async_copy(cols(v_ref, p, HD), vb0.at[p], loc_sem.at[2]),
        pltpu.make_async_copy(cols(g_ref, p, QW), gb.at[p], loc_sem.at[3]),
    ]
    for cp in local:
        cp.start()
    flags[0, 0] = swap_ref[0, 0]

    barrier = pltpu.get_barrier_semaphore()

    def greet(dev):
        pl.semaphore_signal(barrier, inc=1, device_id=dev, device_id_type=MESH)

    inner = jnp.logical_not(first)
    onward = jnp.logical_not(final)
    skip_on = (x >= NX // 2) & onward
    skip_back = (x < NX // 2) & inner
    side_on = (x == 1) & onward
    side_back = (x == 0) & inner
    wrap_on = (x == NX - 1) & onward
    third_back = (x == 2) & inner

    latest = (p == 0) & (c == 0) & (y == 0)
    by_latest = jnp.logical_not(latest) & (((y == 0) & (c <= NX)) | (c == 0))

    @pl.when(jnp.logical_not(latest))
    def _():
        greet((other, c, y))
        for j in range(2):
            for d in range(1, NX):
                greet((j, c - x + lax.rem(x + d, NX), y))
            for d in range(1, n_tp):
                greet((j, c, lax.rem(y + d, n_tp)))
        for cond, dev in (
            (onward, ahead),
            (inner, behind),
            (skip_on, lax.rem(c + 2, n_ctx)),
            (skip_back, lax.rem(c + n_ctx - 2, n_ctx)),
            (side_on, lax.rem(c + 3, n_ctx)),
            (side_back, lax.rem(c + n_ctx - 3, n_ctx)),
            (wrap_on, lax.rem(c + 1, n_ctx)),
            (wrap_on, lax.rem(c + 3, n_ctx)),
            (third_back, lax.rem(c + n_ctx - 3, n_ctx)),
            (side_back, lax.rem(c + n_ctx - 1, n_ctx)),
        ):
            @pl.when(cond)
            def _():
                for j in range(2):
                    greet((j, dev, y))

    met = 1 + 2 * (NX - 1) + 2 * (n_tp - 1) - by_latest.astype(jnp.int32)
    for cond in (onward, inner, skip_on, skip_back, side_on, side_back, wrap_on, side_back, wrap_on, third_back):
        met = met + 2 * cond.astype(jnp.int32)
    pl.semaphore_wait(barrier, met)

    @pl.when(latest)
    def _():
        beside = [(1, 0, 0)]
        for j in range(2):
            beside += [(j, d, 0) for d in range(1, min(NX + 1, n_ctx))]
            beside += [(j, 0, t) for t in range(1, n_tp)]
        for dev in beside:
            pl.semaphore_signal(late_sem, inc=1, device_id=dev, device_id_type=MESH)

    def meet_latest(cond):
        @pl.when(by_latest & cond)
        def _():
            pl.semaphore_wait(late_sem, 1)

    count = [0]
    waits = []

    def remote(src, dst, recv, dev, cond=None):
        sem = send_sem.at[count[0]]
        count[0] += 1
        cp = pltpu.make_async_remote_copy(
            src_ref=src, dst_ref=dst, send_sem=sem, recv_sem=recv,
            device_id=dev, device_id_type=MESH,
        )
        if cond is None:
            cp.start()
        else:
            @pl.when(cond)
            def _():
                cp.start()
        waits.append((cp, cond))
        return cp

    def arrived(ref, sem, cond=None):
        if cond is None:
            pltpu.make_async_copy(ref, ref, sem).wait()
        else:
            @pl.when(cond)
            def _():
                pltpu.make_async_copy(ref, ref, sem).wait()

    mine = (other, c, y)

    def later(d):
        return lax.rem(c + d, n_ctx)

    def earlier(d):
        return lax.rem(c + n_ctx - d, n_ctx)

    def reaches(d):
        return c + 2 < n_ctx if d == 2 else onward if d == REACH else x + d < NX

    def starts(d):
        return (x == 0) | side_on if d == 3 else reaches(d)

    for d in (4, 1, 3, 2):
        remote(flags.at[0], flags.at[d], rf_sem.at[d], (p, later(d), y), starts(d))
    def send(pieces, cond=None):
        for src, dst, sem, d in pieces:
            for j in range(2):
                remote(
                    cols(src, j, HD), dst[d].at[p], sem.at[d], (j, later(d), y),
                    starts(d) if cond is None else cond,
                )

    def send_half(src, dst, sem, h):
        rows = pl.ds(h * (BLK // 2), BLK // 2)
        for j in range(2):
            remote(
                src.at[0, rows, pl.ds(j * HD, HD)], dst.at[p, rows], sem.at[h], (j, ahead, y), onward,
            )

    send_half(k_ref, kb4, rk4_sem, 0)
    send_half(k_ref, kb4, rk4_sem, 1)
    send([(k_ref, kb, rk_sem, 1), (k_ref, kb, rk_sem, 3)])
    send_half(v_ref, vb4, rv4_sem, 0)
    send_half(v_ref, vb4, rv4_sem, 1)
    send([(k_ref, kb, rk_sem, 2)], x < NX // 2)
    send([(v_ref, vb, rv_sem, 1), (v_ref, vb, rv_sem, 3)])
    send([(v_ref, vb, rv_sem, 2)], x < NX // 2)
    meet_latest((y == 0) & (c == 0))
    remote(cols(q_ref, other, QW), qb.at[p], rq_sem.at[0], mine)
    remote(cols(k_ref, other, HD), kb0.at[p], rk_sem.at[0], mine)
    remote(cols(g_ref, other, QW), gb.at[p], rq_sem.at[1], mine)
    remote(cols(v_ref, other, HD), vb0.at[p], rv_sem.at[0], mine)

    for d in range(1, REACH + 1):
        @pl.when(c < d)
        def _():
            flags[d, 0] = 0
            kb[d][...] = jnp.zeros_like(kb[d])
            vb[d][...] = jnp.zeros_like(vb[d])

    lane = lax.broadcasted_iota(jnp.int32, (1, BLK), 1)
    pos = c * BLK + lane
    lows = []
    for pi in range(2):
        low = jnp.maximum(pos - (W - 1), 0)
        end = jnp.int32(0)
        for r in range(len_ref.shape[1]):
            end = end + len_ref[pi, r]
            low = jnp.maximum(low, jnp.where(pos >= end, end, 0))
        lows.append(jnp.concatenate([low] * REP, axis=1) - c * BLK)
    lane2 = jnp.concatenate([lane] * REP, axis=1)
    row_id = lax.broadcasted_iota(jnp.int32, (BLK, QL), 0)

    def pick(ref, swapped, pi):
        a, b = ref[pi], ref[1 - pi]
        return jnp.where(swapped, b, a)

    def take(d):
        swapped = (swap_ref[0, 0] if d == 0 else flags[d, 0]) == 1
        for pi in range(2):
            key = pick(kb[d], swapped, pi)
            ks[pi, d] = key
            s = mm(key, qs[pi], NT) * SCALE
            ok = row_id - d * BLK >= lows[pi]
            if d == 0:
                ok = ok & (row_id <= lane2)
            sc[pi, d] = jnp.where(ok, s, NEGATIVE)

    def take_v(d):
        swapped = (swap_ref[0, 0] if d == 0 else flags[d, 0]) == 1
        for pi in range(2):
            val = pick(vb[d], swapped, pi)
            vs[pi, d] = val
            dp[pi, d] = mm(val, gs[pi], NT)

    def stack(src, dst, swapped):
        for pi in range(2):
            t = pick(src, swapped, pi)
            for r in range(REP):
                dst[pi, r * BLK:(r + 1) * BLK] = t[:, r * HD:(r + 1) * HD]

    for cp in local:
        cp.wait()
    swapped = swap_ref[0, 0] == 1
    arrived(qb.at[other], rq_sem.at[0])
    stack(qb, qs, swapped)
    arrived(kb0.at[other], rk_sem.at[0])
    take(0)
    arrived(gb.at[other], rq_sem.at[1])
    stack(gb, gs, swapped)

    relays = inner & (x >= 2)

    def pass_halves(buf, sem, own_sem):
        for h in range(2):
            rows = pl.ds(h * (BLK // 2), BLK // 2)
            arrived(buf[4].at[:, rows], own_sem.at[h], relays)
            for e in (3, 1):
                remote(
                    buf[4].at[:, rows], buf[4 - e].at[:, rows], sem.at[4 - e],
                    (p, earlier(e), y), inner & (x >= max(e, 2)),
                )
            if h == 0 and own_sem is rk4_sem:
                send([(k_ref, kb, rk_sem, 2), (v_ref, vb, rv_sem, 2)], skip_on)

    def last_halves(buf, own_sem):
        for h in range(2):
            rows = pl.ds(h * (BLK // 2), BLK // 2)
            arrived(buf[4].at[:, rows], own_sem.at[h], inner & (x < 2))

    arrived(flags.at[4], rf_sem.at[4], relays)
    for e in (1, 3):
        remote(flags.at[4], flags.at[4 - e], rf_sem.at[4 - e], (p, earlier(e), y), inner & (x >= max(e, 2)))
    pass_halves(kb, rk_sem, rk4_sem)
    pass_halves(vb, rv_sem, rv4_sem)
    arrived(vb0.at[other], rv_sem.at[0])
    take_v(0)
    for d in (2, 3, 1):
        arrived(flags.at[d], rf_sem.at[d], c >= d)
        arrived(kb[d], rk_sem.at[d], c >= d)
        take(d)
    arrived(flags.at[4], rf_sem.at[4], inner & (x < 2))
    last_halves(kb, rk4_sem)
    take(4)

    def give(s, d, pi):
        straight = d == 1 and s == 0
        direct = c >= d if d == 2 or straight else x >= d
        if d == 3 and s == 0:
            direct = direct | third_back
        remote(part.at[d, s, pi], near.at[d - 1, s, p], pd_sem.at[s, d], (pi, earlier(d), y), direct)
        if d == 3 or (d == 1 and not straight):
            remote(
                part.at[d, s, pi], relay.at[NX - d - 1, s, pi], hub_sem.at[s, pi, NX - d],
                (p, c + NX - d, y), inner & (x < (2 if s == 0 else d)),
            )

    def hand_back(s, pi, cond):
        @pl.when(cond)
        def _():
            part[4, s, pi] = hub[s, pi].astype(jnp.bfloat16)
        remote(part.at[4, s, pi], far.at[s, p], pd_sem.at[s, 4], (pi, behind, y), inner & cond)

    meet_latest((y == 0) & (c > 0))
    for pi in range(2):
        top = jnp.max(sc[pi, 0], axis=0, keepdims=True)
        for d in range(1, REACH + 1):
            top = jnp.maximum(top, jnp.max(sc[pi, d], axis=0, keepdims=True))
        total = jnp.zeros((1, QL), jnp.float32)
        for d in range(REACH + 1):
            e = jnp.exp(sc[pi, d] - top)
            sc[pi, d] = e
            total = total + jnp.sum(e, axis=0, keepdims=True)
        inv = 1.0 / total
        for d in (1, 3, 2, 4, 0):
            pr = sc[pi, d] * inv
            sc[pi, d] = pr
            pb[pi, d] = pr.astype(jnp.bfloat16)
            dv = mm(pb[pi, d], gs[pi], NN)
            if d == 0:
                own[1, pi] = dv
            elif d == 4:
                hub[1, pi] = dv
            else:
                part[d, 1, pi] = dv.astype(jnp.bfloat16)
        for d in (1, 3):
            give(1, d, pi)
        hand_back(1, pi, x < 1)
    for pi in range(2):
        give(1, 2, pi)
    remote(own.at[1, other], mate.at[1], pd_sem.at[1, 0], mine)

    for d in (2, 3, 1):
        arrived(vb[d], rv_sem.at[d], c >= d)
        take_v(d)
    last_halves(vb, rv4_sem)
    take_v(4)
    for pi in range(2):
        delta = jnp.zeros((1, QL), jnp.float32)
        for d in range(REACH + 1):
            delta = delta + jnp.sum(sc[pi, d] * dp[pi, d], axis=0, keepdims=True)
        for d in (1, 3, 2, 4, 0):
            dsb[pi, d] = (sc[pi, d] * (dp[pi, d] - delta)).astype(jnp.bfloat16)
            dk = mm(dsb[pi, d], qs[pi], NN) * SCALE
            if d == 0:
                own[0, pi] = dk
            elif d == 4:
                hub[0, pi] = dk
            else:
                part[d, 0, pi] = dk.astype(jnp.bfloat16)
        for d in (1, 3):
            give(0, d, pi)
        hand_back(0, pi, (x == 0) | (x == NX - 1))
    remote(own.at[0, other], mate.at[0], pd_sem.at[0, 0], mine)

    for pi in range(2):
        o = (mm(dsb[pi].reshape(-1, QL), ks[pi].reshape(-1, HD), TN) * SCALE).astype(jnp.bfloat16)
        for r in range(REP):
            dqb[pi, :, r * HD:(r + 1) * HD] = o[r * BLK:(r + 1) * BLK]
    keep_q = pltpu.make_async_copy(dqb.at[p], cols(gq_ref, p, QW), loc_sem.at[6])
    keep_q.start()
    remote(dqb.at[other], cols(gq_ref, p, QW), out_sem.at[1], mine)
    for pi in range(2):
        give(0, 2, pi)
    for pi in range(2):
        o = mm(pb[pi].reshape(-1, QL), vs[pi].reshape(-1, HD), TN).astype(jnp.bfloat16)
        for r in range(REP):
            ob[pi, :, r * HD:(r + 1) * HD] = o[r * BLK:(r + 1) * BLK]
    meet_latest(y > 0)
    share = BLK // n_tp
    width = REP * HD
    at = pl.ds(pl.multiple_of((y * 2 + p) * width, width), width)
    for dt in range(n_tp):
        t = lax.rem(y + dt, n_tp)
        rows = pl.ds(pl.multiple_of(t * share, share), share)
        for dj in range(2):
            pi = p if dj == 0 else other
            if dt == 0 and dj == 0:
                keep = pltpu.make_async_copy(ob.at[pi, rows], ao_ref.at[0, :, at], loc_sem.at[5])
                keep.start()
            else:
                remote(ob.at[pi, rows], ao_ref.at[0, :, at], out_sem.at[0], (pi, c, t))

    for s in (1, 0):
        for pi in range(2):
            for e in (1, 3):
                if s == 0 and e == 3:
                    continue

                @pl.when(inner & (x >= e) & (x < (NX - 1 if s == 0 else NX)))
                def _():
                    arrived(relay.at[e - 1, s, pi], hub_sem.at[s, pi, e])
                    hub[s, pi] = hub[s, pi] + relay[e - 1, s, pi].astype(jnp.float32)
            hand_back(s, pi, (x >= 1) & (x < (NX - 1 if s == 0 else NX)))

    for s, out in ((1, gv_ref), (0, gk_ref)):
        arrived(mate.at[s], pd_sem.at[s, 0])
        for d in range(1, NX):
            @pl.when(reaches(d) | (wrap_on if d != 2 and s == 0 else reaches(d)))
            def _():
                arrived(near.at[d - 1, s], pd_sem.at[s, d])
                own[s, p] = own[s, p] + near[d - 1, s, p].astype(jnp.float32)
                mate[s] = mate[s] + near[d - 1, s, other].astype(jnp.float32)

        @pl.when(onward)
        def _():
            arrived(far.at[s], pd_sem.at[s, 4])
            own[s, p] = own[s, p] + far[s, p].astype(jnp.float32)
            mate[s] = mate[s] + far[s, other].astype(jnp.float32)
        for j, src in ((p, own[s, p]), (other, mate[s])):
            out[0, :, pl.ds(pl.multiple_of(j * HD, HD), HD)] = src.astype(jnp.bfloat16)

    keep.wait()
    keep_q.wait()
    arrived(ao_ref.at[0, :, pl.ds(0, (2 * n_tp - 1) * width)], out_sem.at[0])
    arrived(cols(gq_ref, other, QW), out_sem.at[1])
    for cp, cond in waits:
        if cond is None:
            cp.wait_send()
        else:
            @pl.when(cond)
            def _():
                cp.wait_send()


def store(a_ref, b_ref, c_ref, d_ref, ao_ref, gq_ref, gk_ref, gv_ref, sem):
    copies = [
        pltpu.make_async_copy(src, dst, sem.at[i])
        for i, (src, dst) in enumerate(((a_ref, ao_ref), (b_ref, gq_ref), (c_ref, gk_ref), (d_ref, gv_ref)))
    ]
    for cp in copies:
        cp.start()
    for cp in copies:
        cp.wait()


def body(n_ctx, n_tp, queries, key_rows, values, grad_out, lengths, pair_swap):
    bf, f32 = jnp.bfloat16, jnp.float32
    nd = REACH + 1
    kv_piece = pltpu.VMEM((2, BLK, HD), bf)
    any_spec = pl.BlockSpec(memory_space=pl.ANY)
    vmem_spec = pl.BlockSpec(memory_space=pltpu.VMEM)
    dma = pltpu.SemaphoreType.DMA
    shapes = (
        ((1, BLK // n_tp, n_tp * 2 * QW), bf),
        (queries.shape, bf),
        (key_rows.shape, bf),
        (values.shape, bf),
    )
    held = pl.pallas_call(
        functools.partial(kernel, n_ctx, n_tp),
        out_shape=tuple(pltpu.VMEM(*item) for item in shapes),
        in_specs=[any_spec] * 4 + [pl.BlockSpec(memory_space=pltpu.SMEM)] * 2,
        out_specs=(vmem_spec,) * 4,
        scratch_shapes=[kv_piece] * 10 + [
            pltpu.VMEM((2, BLK, QW), bf),
            pltpu.VMEM((2, BLK, QW), bf),
            pltpu.SMEM((nd, 1), jnp.int32),
            pltpu.VMEM((2, nd, BLK, HD), bf),
            pltpu.VMEM((2, nd, BLK, HD), bf),
            pltpu.VMEM((2, QL, HD), bf),
            pltpu.VMEM((2, QL, HD), bf),
            pltpu.VMEM((2, nd, BLK, QL), f32),
            pltpu.VMEM((2, nd, BLK, QL), f32),
            pltpu.VMEM((2, nd, BLK, QL), bf),
            pltpu.VMEM((2, nd, BLK, QL), bf),
            pltpu.VMEM((2, BLK, QW), bf),
            pltpu.VMEM((2, BLK, QW), bf),
            pltpu.VMEM((nd, 2, 2, BLK, HD), bf),
            pltpu.VMEM((2, 2, BLK, HD), f32),
            pltpu.VMEM((2, BLK, HD), f32),
            pltpu.VMEM((3, 2, 2, BLK, HD), bf),
            pltpu.VMEM((2, 2, BLK, HD), bf),
            pltpu.VMEM((2, 2, BLK, HD), f32),
            pltpu.VMEM((3, 2, 2, BLK, HD), bf),
            dma((7,)),
            dma((2,)),
            dma((2,)),
            pltpu.SemaphoreType.REGULAR,
            dma((100,)),
            dma((nd,)),
            dma((nd,)),
            dma((2,)),
            dma((nd,)),
            dma((2,)),
            dma((2, nd)),
            dma((2, 2, NX)),
        ],
        compiler_params=pltpu.CompilerParams(collective_id=0, has_side_effects=True),
        name="attend",
    )(queries, key_rows, values, grad_out, lengths, pair_swap.reshape(1, 1))
    return pl.pallas_call(
        store,
        out_shape=tuple(jax.ShapeDtypeStruct(*item) for item in shapes),
        in_specs=[any_spec] * 4,
        out_specs=(any_spec,) * 4,
        scratch_shapes=[dma((4,))],
        name="store",
    )(*[pltpu.with_memory_space_constraint(item, pltpu.VMEM) for item in held])


def solution(mesh):
    placed = P("dp", "ctx", "tp")
    return jax.shard_map(
        functools.partial(body, mesh.shape["ctx"], mesh.shape["tp"]),
        mesh=mesh,
        in_specs=(placed, placed, placed, placed, P(), P("ctx")),
        out_specs=(P("dp", ("ctx", "tp"), None), placed, placed, placed),
        check_vma=False,
    )
```
